128 devices in a mesh: region: 8 (over z, core), tile: 16 (over y, x).
Axes of the slice: x: 4, y: 4, z: 4, core: 2. Of those that a mesh axis runs over, the one named last changes fastest.
Arguments:
- global_deriv: bfloat16 [24576, 32, 128], P(('region', 'tile')), may hold values from -0.109375 to 0.109375
- local_deriv: bfloat16 [24576, 5, 32], P(('region', 'tile')), may hold values from -4 to 4
- hit_weight: bfloat16 [24576, 32], P(('region', 'tile')), may hold values from 0.25 to 4
- hit_resid: bfloat16 [24576, 32], P(('region', 'tile')), may hold values from -6 to 6
- block_ids: int32 [24576, 32], P(('region', 'tile')), may hold values from 0 to 7
- hit_count: int32 [24576], P(('region', 'tile')), may hold values from 4 to 32
- track_region: int32 [24576, 1], P(('region', 'tile')), may hold values from 0 to 7; in each aligned block of 192 rows (0 to 191, 192 to 383, ...) at most 48 rows name the same one
- block_place: int32 [8], replicated, may hold values from 0 to 7, each once
Outputs:
- normal_matrix: float32 [8, 1024, 1024], P('region', 'tile')
- right_side: float32 [8, 1024], P('region', 'tile')
The draws below stay inside these ranges and needn't reach their ends.
Inputs may be any that keep to these rules, and one draw needn't show every extreme that they name: `track_region`: among the tracks of one device at most 48 share a region, and in every draw some device has exactly 48 tracks in some region. `block_place`: each position appears once.
All inputs are finite; a program needn't handle non-finite values.
Results may differ from the reference program's by a relative error of at most 0.0029.
Values may be sent and summed in bfloat16 or wider, within the bound.
A program may use at most 128 MiB of HBM per device.

```python
import math
import jax
import jax.numpy as jnp
import numpy as np
from jax import lax

BS = 128
BR = 8
HITS = 32
TRK_DEV = 192
CAP = 48
TRACKS = 24576
N_REGION = 8
N_TILE = 16


def place_ends(array, rng, least, largest):
    spot = [jax.random.randint(jax.random.fold_in(rng, axis), (), 0, length) for axis, length in enumerate(array.shape)]
    longest = array.shape.index(max(array.shape))
    next_to = spot[:longest] + [(spot[longest] + 1) % array.shape[longest]] + spot[longest + 1:]
    return array.at[tuple(spot)].set(least).at[tuple(next_to)].set(largest)


def shard_levels(rng, shape, split, least, largest):
    factor_of = 1.0
    for position, shards_of in split:
        draws = jax.random.uniform(jax.random.fold_in(jax.random.fold_in(rng, 6), position), (shards_of,), jnp.float32, least / len(split), largest / len(split))
        factor_of = factor_of * jnp.repeat(jnp.exp(draws), shape[position] // shards_of).reshape((-1,) + (1,) * (len(shape) - 1 - position))
    return factor_of


def routed_block(stream_key, own, number, rows, count, top, reach, skew):
    order = jax.random.permutation(stream_key, count)
    heavy_load, common = portions_of(count, rows * top, reach, skew, True), portions_of(count, rows * top, reach, skew, False)
    places = jnp.arange(count)

    def named(lengths, offset_by):
        used = int((lengths > 0).sum())
        fixed = max(1, used // 4)
        passed = fixed + (places - fixed + offset_by * (used - fixed)) % max(1, count - fixed)
        return jnp.zeros((count,), jnp.int32).at[order[jnp.where(places < fixed, places, passed)]].set(jnp.asarray(lengths, jnp.int32))

    lengths = jnp.where(number % 4 == 0, named(heavy_load, number // 4), named(common, number - number // 4 - 1))
    mixed = jax.random.permutation(jax.random.fold_in(own, 3), count)
    giver, sink = mixed[0:count // 2 * 2:2], mixed[1:count // 2 * 2:2]
    slack = jnp.minimum(lengths[giver] - 1, reach - lengths[sink]) // 2
    slack = jnp.where((giver == order[0]) | (sink == order[0]) | (lengths[sink] == 0), 0, jnp.maximum(slack, 0))
    passed = jax.random.randint(jax.random.fold_in(own, 4), (count // 2,), 0, 1 << 20) % (slack + 1)
    lengths = lengths.at[giver].add(-passed).at[sink].add(passed)
    members = jnp.searchsorted(jnp.cumsum(lengths), jnp.arange(rows * top), side="right").astype(jnp.int32)
    listing = members.reshape(top, rows).T
    listing = listing[jax.random.permutation(jax.random.fold_in(own, 1), rows)]
    offset_by = jax.random.randint(jax.random.fold_in(own, 2), (rows, 1), 0, top)
    return jnp.take_along_axis(listing, (jnp.arange(top)[None, :] + offset_by) % top, axis=1)


def portions_of(amount, total, most, skew, full):
    weights = [(1 << 20) // math.isqrt(grade ** skew) + 1 for grade in range(1, amount + 1)]
    largest = most if full else min(most, max(-(-total // amount), total * weights[0] // sum(weights)))
    least = 1 if total - largest >= amount - 1 else 0
    holding, surplus = [largest] + [least] * (amount - 1), total - largest - least * (amount - 1)
    while surplus > 0:
        free = [i for i in range(1, amount) if holding[i] < largest] or [i for i in range(1, amount) if holding[i] < most]
        whole, budget = sum([weights[i] for i in free]), surplus
        for i in free:
            more = min(most - holding[i], max(1, budget * weights[i] // whole), surplus)
            holding[i] = holding[i] + more
            surplus = surplus - more
    return np.array(holding)


def noise(key, extent, deviation, most, split=(), kind=jnp.bfloat16):
    factor_of = shard_levels(key, extent, split, -0.22, 0.18) if split else 1.0
    array = jax.random.normal(key, extent, jnp.float32) * deviation * factor_of
    return jnp.minimum(jnp.maximum(array, -most), most).astype(kind)


def setup_inputs(seed: int = 0) -> dict:
    splits = jax.random.split(jax.random.key(seed), 9)
    global_deriv = noise(splits[0], (TRACKS, HITS, BS), (TRK_DEV * N_TILE) ** -0.5, 0.109375, ((0, 128),))
    local_deriv = noise(splits[1], (TRACKS, 5, HITS), 1.0, 4.0, ((0, 128),))
    hit_weight = jnp.clip(jnp.exp(math.log(4.0) - 2.7725887 * jax.random.uniform(splits[2], (TRACKS, HITS), jnp.float32) ** shard_levels(splits[2], (TRACKS, HITS), ((0, 128),), -0.2, 0.2)), 0.25, 4.0).astype(jnp.bfloat16)
    hit_resid = noise(splits[3], (TRACKS, HITS), 1.0, 6.0, ((0, 128),))
    block_ids = place_ends(jax.random.randint(splits[4], (TRACKS, HITS), 0, BR), jax.random.fold_in(splits[4], 1), 0, BR - 1).astype(jnp.int32)
    hit_count = place_ends(jax.random.randint(splits[5], (TRACKS,), 4, HITS + 1), jax.random.fold_in(splits[5], 1), 4, HITS).astype(jnp.int32)
    track_region_keys = jax.random.split(jax.random.fold_in(splits[6], 1), TRACKS // TRK_DEV)
    track_region_turns = jax.random.permutation(jax.random.fold_in(splits[6], 3), TRACKS // TRK_DEV)
    track_region = jax.vmap(lambda own, number: routed_block(jax.random.fold_in(splits[6], 2), own, number, TRK_DEV, N_REGION, 1, CAP, 2))(track_region_keys, track_region_turns).reshape((TRACKS, 1))
    block_place = jax.random.permutation(splits[7], BR).astype(jnp.int32)
    return dict(global_deriv=global_deriv, local_deriv=local_deriv, hit_weight=hit_weight, hit_resid=hit_resid, block_ids=block_ids, hit_count=hit_count, track_region=track_region, block_place=block_place)


def cholesky_fit(local_slopes, weight, misfit, live_hits):
    masked_w = live_hits * weight
    weighted_l = local_slopes * masked_w[:, None, :]
    gamma_mat = [[lax.optimization_barrier(jnp.sum(weighted_l[:, a, :] * local_slopes[:, b, :], axis=1)) + (1.0 if a == b else 0.0) for b in range(5)] for a in range(5)]
    beta_vec = [lax.optimization_barrier(jnp.sum(weighted_l[:, a, :] * misfit, axis=1)) for a in range(5)]
    factor = [[None for b in range(5)] for a in range(5)]
    for j in range(5):
        center = gamma_mat[j][j]
        for k in range(j):
            center = center - factor[j][k] * factor[j][k]
        factor[j][j] = jnp.sqrt(center)
        for i in range(j + 1, 5):
            offdiag = gamma_mat[i][j]
            for k in range(j):
                offdiag = offdiag - factor[i][k] * factor[j][k]
            factor[i][j] = offdiag / factor[j][j]
    solved = []
    solved_rhs = []
    for j in range(5):
        current = weighted_l[:, j, :]
        target = beta_vec[j]
        for k in range(j):
            current = current - factor[j][k][:, None] * solved[k]
            target = target - factor[j][k] * solved_rhs[k]
        solved.append(current / factor[j][j][:, None])
        solved_rhs.append(target / factor[j][j])
    scaled = jnp.stack(solved, axis=1)
    projection = solved[0] * solved_rhs[0][:, None]
    for k in range(1, 5):
        projection = projection + solved[k] * solved_rhs[k][:, None]
    hit_factor = masked_w * misfit - projection
    return (scaled, hit_factor, masked_w)

def fit_tracks(gderiv, packed, block_rows, counts, place):
    hit_slots = block_rows.shape[1]
    blocks = place.shape[0]
    live_hits = (jnp.arange(hit_slots)[None, :] < counts[:, None]).astype(jnp.float32)
    floats = packed.astype(jnp.float32)
    scaled, hit_factor, masked_w = cholesky_fit(floats[:, 0:5, :], floats[:, 5, :], floats[:, 6, :], live_hits)
    matches = (block_rows[:, :, None] == jnp.arange(blocks)[None, None, :]).astype(jnp.float32)
    placing = (place[:, None] == jnp.arange(blocks)[None, :]).astype(jnp.float32)
    onehot = jnp.einsum('nhb,bp->nhp', matches, placing, precision=lax.Precision.HIGHEST)
    gfloat = gderiv.astype(jnp.float32)
    expanded = scaled[:, :, :, None] * onehot[:, None, :, :]
    spread = jnp.einsum('nchp,nhi->ncpi', expanded, gfloat, precision=lax.Precision.HIGHEST).astype(jnp.bfloat16)
    weighted = (masked_w[:, :, None] * gfloat).astype(jnp.bfloat16)
    return (spread, weighted, hit_factor.astype(jnp.bfloat16), onehot)

def place_direct(weighted, gderiv, onehot):
    blocks = onehot.shape[2]
    block_size = gderiv.shape[2]
    flat_g = gderiv.reshape(-1, block_size)
    diagonal_part = jnp.zeros((blocks * block_size, blocks * block_size), jnp.float32)
    for column in range(blocks):
        picked = (weighted * onehot[:, :, column, None].astype(jnp.bfloat16)).reshape(-1, block_size)
        tile_sum = lax.dot_general(picked, flat_g, (((0,), (0,)), ((), ())), preferred_element_type=jnp.float32)
        diagonal_part = diagonal_part.at[column * block_size:(column + 1) * block_size, column * block_size:(column + 1) * block_size].set(tile_sum)
    return diagonal_part

def right_vector(hit_factor, gderiv, onehot):
    block_size = gderiv.shape[2]
    loads = (hit_factor[:, :, None] * onehot.astype(jnp.bfloat16)).reshape(-1, onehot.shape[2])
    summed = lax.dot_general(loads, gderiv.reshape(-1, block_size), (((0,), (0,)), ((), ())), preferred_element_type=jnp.float32)
    return summed.reshape(-1)

def reference(global_deriv, local_deriv, hit_weight, hit_resid, block_ids, hit_count, track_region, block_place):
    owning = track_region[:, 0]
    bound = N_REGION * N_TILE * CAP
    packed_all = jnp.concatenate([local_deriv, hit_weight[:, None, :], hit_resid[:, None, :]], axis=1)
    slab_width = BR * BS

    def region_term(index):
        inside = owning == index
        chosen = jnp.nonzero(inside, size=bound, fill_value=0)[0].astype(jnp.int32)
        total = jnp.sum(inside.astype(jnp.int32))
        filled = (jnp.arange(bound) < total).astype(jnp.int32)
        gderiv = jnp.take(global_deriv, chosen, axis=0)
        packed = jnp.take(packed_all, chosen, axis=0)
        block_rows = jnp.take(block_ids, chosen, axis=0)
        counts = jnp.take(hit_count, chosen, axis=0) * filled
        spread, weighted, hit_factor, onehot = fit_tracks(gderiv, packed, block_rows, counts, block_place)
        flat_spread = spread.reshape(-1, slab_width)
        schur = jnp.dot(flat_spread.T, flat_spread, preferred_element_type=jnp.float32)
        diagonal_part = place_direct(weighted, gderiv, onehot)
        return (diagonal_part - schur, right_vector(hit_factor, gderiv, onehot))
    normal_matrix, right_side = lax.map(region_term, jnp.arange(N_REGION).astype(jnp.int32))
    return (normal_matrix, right_side)
```

```python
import functools

import jax
import jax.numpy as jnp
from jax import lax
from jax.experimental import pallas as pl
from jax.experimental.pallas import tpu as pltpu
from jax.sharding import PartitionSpec as P

BS = 128
BR = 8
HITS = 32
TRK = 192
CAP = 48
N_REGION = 8
HALF = CAP // 2
GROUP = 8
CHUNKS = 16
ROWS = 64
WIDTH = BR * BS
F32 = jnp.float32
BF16 = jnp.bfloat16
DIRS = (
    (1, 0, 0, 1, 0),
    (0, 0, 1, 1, 1),
    (-1, 0, 0, 3, 0),
    (0, 0, -1, 3, 1),
    (0, 1, 0, 2, 0),
    (0, -1, 0, 2, 1),
)


def fit(aux_ref):
    t = jnp.transpose(aux_ref[...].astype(F32))
    slopes = [t[32 * c : 32 * c + 32] for c in range(5)]
    w, r, place = t[160:192], t[192:224], t[224:256]
    wl = [s * w for s in slopes]
    gamma = [[None] * 5 for _ in range(5)]
    for a in range(5):
        for b in range(a + 1):
            gamma[a][b] = jnp.sum(wl[a] * slopes[b], axis=0, keepdims=True) + (1.0 if a == b else 0.0)
    beta = [jnp.sum(wl[a] * r, axis=0, keepdims=True) for a in range(5)]
    factor = [[None] * 5 for _ in range(5)]
    inverse = [None] * 5
    for j in range(5):
        center = gamma[j][j]
        for k in range(j):
            center = center - factor[j][k] * factor[j][k]
        factor[j][j] = jnp.sqrt(center)
        inverse[j] = 1.0 / factor[j][j]
        for i in range(j + 1, 5):
            off = gamma[i][j]
            for k in range(j):
                off = off - factor[i][k] * factor[j][k]
            factor[i][j] = off * inverse[j]
    solved, target = [], []
    for j in range(5):
        cur, tgt = wl[j], beta[j]
        for k in range(j):
            cur = cur - factor[j][k] * solved[k]
            tgt = tgt - factor[j][k] * target[k]
        solved.append(cur * inverse[j])
        target.append(tgt * inverse[j])
    hit = w * r
    for k in range(5):
        hit = hit - solved[k] * target[k]
    full = jnp.concatenate(solved + [hit, w, place], axis=0)
    return jnp.transpose(full).astype(BF16)


def kernel(
    idx_ref, g_ref, aux_ref, slot_ref,
    out_ref, vec_ref,
    gsend, grecv, asend, arecv, fitted, lhs, s_buf, d_acc, v_acc, psend, precv, vrecv,
    gs_sem, gr_sem, as_sem, ar_sem, ps_sem, pr_sem, vs_sem, vr_sem,
):
    region = lax.axis_index("region")
    tile = lax.axis_index("tile")
    z, core = region // 2, region % 2
    y, x = tile // 4, tile % 4
    colour = (x + 2 * y + z) % 4

    def device(nx, ny, nz, ncore):
        return {"region": nz * 2 + ncore, "tile": ny * 4 + nx}

    def neighbour(d, ncore):
        dx, dy, dz = DIRS[d][:3]
        return device((x + dx + 4) % 4, (y + dy + 4) % 4, (z + dz + 4) % 4, ncore)

    sibling = device(x, y, z, 1 - core)

    barrier = pltpu.get_barrier_semaphore()
    for d in range(6):
        for c in range(2):
            pl.semaphore_signal(barrier, inc=1, device_id=neighbour(d, c))
    pl.semaphore_signal(barrier, inc=1, device_id=sibling)

    def worker_of(i, rz):
        wy, wx = i // 4, i % 4
        return {"region": ((rz - wx - 2 * wy + 12) % 4) * 2 + core, "tile": i}

    own_worker = (x + 2 * y) % 4 == 0

    def greet(i, carry):
        @pl.when(jnp.logical_not(jnp.logical_and(own_worker, i == tile)))
        def _():
            pl.semaphore_signal(barrier, inc=1, device_id=worker_of(i, z))
        return carry

    lax.fori_loop(0, 16, greet, 0)
    pl.semaphore_wait(barrier, jnp.where(own_worker, 28, 29))

    def gather(q, ref, k):
        def body(i, carry):
            ref[k, i] = g_ref[idx_ref[q * HALF + i]]
            return carry
        lax.fori_loop(0, HALF, body, 0, unroll=4)

    def chunk_of(d, c):
        step, half = DIRS[d][3:]
        return (((colour + step) % 4) * 2 + c) * 2 + half

    def g_copy(d, c):
        k = d * 2 + c
        return pltpu.make_async_remote_copy(
            src_ref=gsend.at[k], dst_ref=grecv.at[d * 2 + core],
            send_sem=gs_sem.at[k], recv_sem=gr_sem.at[d * 2 + core],
            device_id=neighbour(d, c))

    def a_copy(d, c):
        k = d * 2 + c
        return pltpu.make_async_remote_copy(
            src_ref=asend.at[k], dst_ref=arecv.at[d * 2 + core],
            send_sem=as_sem.at[k], recv_sem=ar_sem.at[d * 2 + core],
            device_id=neighbour(d, c))

    def g_sib(h):
        return pltpu.make_async_remote_copy(
            src_ref=gsend.at[12 + h], dst_ref=grecv.at[12 + 2 * core + h],
            send_sem=gs_sem.at[12 + h], recv_sem=gr_sem.at[12 + 2 * core + h],
            device_id=sibling)

    def a_sib(h):
        return pltpu.make_async_remote_copy(
            src_ref=asend.at[12 + h], dst_ref=arecv.at[12 + 2 * core + h],
            send_sem=as_sem.at[12 + h], recv_sem=ar_sem.at[12 + 2 * core + h],
            device_id=sibling)

    for d in range(6):
        for c in range(2):
            gather(chunk_of(d, c), gsend, d * 2 + c)
            g_copy(d, c).start()
    for h in range(2):
        gather((colour * 2 + 1 - core) * 2 + h, gsend, 12 + h)
        g_sib(h).start()
    for h in range(2):
        gather((colour * 2 + core) * 2 + h, grecv, 12 + 2 * core + h)

    fitted[...] = fit(aux_ref)
    slot = slot_ref[...]

    def pick(q):
        rows = q * HALF + lax.broadcasted_iota(jnp.int32, (HALF, 256), 0)
        onehot = jnp.where(slot == rows, 1.0, 0.0).astype(BF16)
        return jnp.dot(onehot, fitted[...], preferred_element_type=F32).astype(BF16)

    for d in range(6):
        for c in range(2):
            asend[d * 2 + c] = pick(chunk_of(d, c))
            a_copy(d, c).start()
    for h in range(2):
        asend[12 + h] = pick((colour * 2 + 1 - core) * 2 + h)
        a_sib(h).start()
    for h in range(2):
        arecv[12 + 2 * core + h] = pick((colour * 2 + core) * 2 + h)

    d_acc[...] = jnp.zeros_like(d_acc)
    v_acc[...] = jnp.zeros_like(v_acc)

    lane = lax.broadcasted_iota(jnp.int32, (GROUP, 128), 1)
    track = lax.broadcasted_iota(jnp.int32, (GROUP, 128), 0)
    residue = track % 4
    blocks = [(lane // HITS + 4 * v) == track for v in range(2)]
    subf = lax.broadcasted_iota(jnp.int32, (GROUP, 256), 0).astype(F32)

    def chunk(m, carry):
        n = jnp.where(m < 2, 12 + 2 * core + m, jnp.where(m < 4, 12 + 2 * (1 - core) + m - 2, m - 4))

        @pl.when(m >= 2)
        def _():
            pltpu.make_async_remote_copy(
                src_ref=gsend.at[0], dst_ref=grecv.at[n], send_sem=gs_sem.at[0],
                recv_sem=gr_sem.at[n], device_id=sibling).wait_recv()
            pltpu.make_async_remote_copy(
                src_ref=asend.at[0], dst_ref=arecv.at[n], send_sem=as_sem.at[0],
                recv_sem=ar_sem.at[n], device_id=sibling).wait_recv()

        a = arecv[n].astype(F32)
        g = grecv[n].reshape(HALF * HITS, BS)
        gt = jnp.transpose(g)
        parts, wps = [], []
        vec = None
        for j in range(3):
            aj = a[GROUP * j : GROUP * j + GROUP]

            turned = []
            for v in range(2):
                half = aj[:, 128 * v : 128 * v + 128]
                turned.append([half] + [pltpu.roll(half, HITS * k, 1) for k in range(1, 4)])

            def spread_lanes(q):
                options = turned[q // 4]
                own_turn = options[(3 - q) % 4]
                for k in range(3):
                    own_turn = jnp.where(residue == k, options[(k - q) % 4], own_turn)
                return jnp.concatenate([jnp.where(b, own_turn, 0.0) for b in blocks], axis=1)

            place = spread_lanes(7)
            base = [spread_lanes(q) for q in range(5)]
            rows = []
            for p in range(BR):
                here = place == float(p)
                rows.extend(jnp.where(here, b, 0.0) for b in base)
            left = jnp.concatenate(rows, axis=0).astype(BF16)
            gj = g[256 * j : 256 * j + 256]
            parts.append(jnp.dot(left, gj, preferred_element_type=F32))
            prow = jnp.sum(place, axis=0, keepdims=True)
            hrow = jnp.sum(spread_lanes(5), axis=0, keepdims=True)
            wrow = jnp.sum(spread_lanes(6), axis=0, keepdims=True)
            onp = subf == prow
            vj = jnp.dot(jnp.where(onp, hrow, 0.0).astype(BF16), gj, preferred_element_type=F32)
            vec = vj if vec is None else vec + vj
            wps.append(jnp.where(onp, wrow, 0.0).astype(BF16))
        v_acc[...] += vec
        wp = jnp.concatenate(wps, axis=1)
        pad = jnp.zeros((8, BS), F32)
        for p in range(BR):
            piece = jnp.concatenate([q[40 * p : 40 * p + 40] for q in parts] + [pad], axis=0)
            s_buf[pl.ds(pl.multiple_of(m * 128, 128), 128), BS * p : BS * p + BS] = piece.astype(BF16)
            lhs[BS * p : BS * p + BS, :] = gt * wp[p : p + 1, :]
        d_acc[...] += jnp.dot(lhs[...], g, preferred_element_type=F32)
        return carry

    lax.fori_loop(0, CHUNKS, chunk, 0)

    def p_copy(i):
        return pltpu.make_async_remote_copy(
            src_ref=psend.at[i], dst_ref=precv.at[tile],
            send_sem=ps_sem.at[i], recv_sem=pr_sem.at[tile],
            device_id={"region": colour * 2 + core, "tile": i})

    def v_copy(i):
        return pltpu.make_async_remote_copy(
            src_ref=v_acc, dst_ref=vrecv.at[tile],
            send_sem=vs_sem.at[i], recv_sem=vr_sem.at[tile],
            device_id={"region": colour * 2 + core, "tile": i})

    def is_self(i):
        return jnp.logical_and(own_worker, i == tile)

    def piece(a, carry):
        cols = pl.ds(pl.multiple_of(a * 256, 256), 256)
        prod = lax.dot_general(
            s_buf[:, cols], s_buf[...], (((0,), (0,)), ((), ())), preferred_element_type=F32)
        lhs_cols = lax.broadcasted_iota(jnp.int32, (1, WIDTH), 1) // BS
        for e in range(2):
            dblock = d_acc[pl.ds(pl.multiple_of(a * 256 + e * 128, 128), 128), :]
            wide = jnp.concatenate([dblock] * BR, axis=1)
            part = jnp.where(lhs_cols == a * 2 + e, wide, 0.0) - prod[e * 128 : e * 128 + 128]
            part = part.astype(BF16)
            for u in range(2):
                psend[a * 4 + e * 2 + u] = part[ROWS * u : ROWS * u + ROWS]
        for u in range(4):
            i = a * 4 + u

            @pl.when(jnp.logical_not(is_self(i)))
            def _():
                p_copy(i).start()
                v_copy(i).start()

            @pl.when(is_self(i))
            def _():
                precv[tile] = psend[i]
                vrecv[tile] = v_acc[...]
        return carry

    lax.fori_loop(0, 4, piece, 0)

    def collect(i, carry):
        @pl.when(jnp.logical_not(is_self(i)))
        def _():
            pltpu.make_async_remote_copy(
                src_ref=psend.at[0], dst_ref=precv.at[i], send_sem=ps_sem.at[0],
                recv_sem=pr_sem.at[i], device_id=sibling).wait_recv()
            pltpu.make_async_remote_copy(
                src_ref=v_acc, dst_ref=vrecv.at[i], send_sem=vs_sem.at[0],
                recv_sem=vr_sem.at[i], device_id=sibling).wait_recv()
        return carry

    lax.fori_loop(0, 16, collect, 0)

    total = precv[0].astype(F32)
    vtot = vrecv[0]
    for i in range(1, 16):
        total = total + precv[i].astype(F32)
        vtot = vtot + vrecv[i]
    out_ref[0] = total
    mine = lax.broadcasted_iota(jnp.int32, (BR, BS), 0) == tile // 2
    row = jnp.sum(jnp.where(mine, vtot, 0.0), axis=0, keepdims=True)
    vec_ref[...] = jnp.where(tile % 2 == 0, row[:, :ROWS], row[:, ROWS:])

    for d in range(6):
        for c in range(2):
            g_copy(d, c).wait_send()
            a_copy(d, c).wait_send()
    for h in range(2):
        g_sib(h).wait_send()
        a_sib(h).wait_send()

    def finish(i, carry):
        @pl.when(jnp.logical_not(is_self(i)))
        def _():
            p_copy(i).wait_send()
            v_copy(i).wait_send()
        return carry

    lax.fori_loop(0, 16, finish, 0)


def local(
    global_deriv,
    local_deriv,
    hit_weight,
    hit_resid,
    block_ids,
    hit_count,
    track_region,
    block_place,
):
    own = track_region[:, 0]
    order = jnp.arange(TRK)
    before = (own[:, None] == own[None, :]) & (order[None, :] < order[:, None])
    slot = own * CAP + jnp.sum(before.astype(jnp.int32), axis=1)
    slots = jnp.arange(N_REGION * CAP)
    index = jnp.sum(jnp.where(slot[None, :] == slots[:, None], order[None, :], 0), axis=1).astype(jnp.int32)
    live = jnp.arange(HITS)[None, :] < hit_count[:, None]
    weight = jnp.where(live, hit_weight, jnp.zeros_like(hit_weight))
    place = jnp.zeros(block_ids.shape, jnp.int32)
    for b in range(BR):
        place = place + jnp.where(block_ids == b, block_place[b], 0)
    aux = jnp.concatenate(
        [local_deriv.reshape(TRK, 5 * HITS), weight, hit_resid, place.astype(BF16)], axis=1)
    aux = jnp.pad(aux, ((0, 256 - TRK), (0, 0)))
    slot_row = jnp.pad(slot.astype(jnp.int32), (0, 256 - TRK), constant_values=-1)[None, :]
    vmem = pl.BlockSpec(memory_space=pltpu.VMEM)
    dma = pltpu.SemaphoreType.DMA
    return pl.pallas_call(
        kernel,
        name="assemble",
        out_shape=(
            jax.ShapeDtypeStruct((1, ROWS, WIDTH), F32),
            jax.ShapeDtypeStruct((1, ROWS), F32),
        ),
        in_specs=[pl.BlockSpec(memory_space=pltpu.SMEM), vmem, vmem, vmem],
        out_specs=(vmem, vmem),
        scratch_shapes=[
            pltpu.VMEM((14, HALF, HITS, BS), BF16),
            pltpu.VMEM((CHUNKS, HALF, HITS, BS), BF16),
            pltpu.VMEM((14, HALF, 256), BF16),
            pltpu.VMEM((CHUNKS, HALF, 256), BF16),
            pltpu.VMEM((256, 256), BF16),
            pltpu.VMEM((WIDTH, HALF * HITS), BF16),
            pltpu.VMEM((CHUNKS * 128, WIDTH), BF16),
            pltpu.VMEM((WIDTH, BS), F32),
            pltpu.VMEM((BR, BS), F32),
            pltpu.VMEM((16, ROWS, WIDTH), BF16),
            pltpu.VMEM((16, ROWS, WIDTH), BF16),
            pltpu.VMEM((16, BR, BS), F32),
            dma((14,)), dma((16,)), dma((14,)), dma((16,)),
            dma((16,)), dma((16,)), dma((16,)), dma((16,)),
        ],
        compiler_params=pltpu.CompilerParams(
            collective_id=0, has_side_effects=True, vmem_limit_bytes=56 << 20),
    )(index, global_deriv, aux, slot_row)


def solution(mesh):
    return jax.shard_map(
        local,
        mesh=mesh,
        in_specs=(
            P(("region", "tile"), None, None),
            P(("region", "tile"), None, None),
            P(("region", "tile"), None),
            P(("region", "tile"), None),
            P(("region", "tile"), None),
            P(("region", "tile")),
            P(("region", "tile"), None),
            P(),
        ),
        out_specs=(P("region", "tile", None), P("region", "tile")),
        check_vma=False,
    )
```

```python
import functools

import jax
import jax.numpy as jnp
from jax import lax
from jax.experimental import pallas as pl
from jax.experimental.pallas import tpu as pltpu
from jax.sharding import PartitionSpec as P

BS = 128
BR = 8
HITS = 32
TRK = 192
CAP = 48
N_REGION = 8
HALF = CAP // 2
GROUP = 8
CHUNKS = 16
ROWS = 64
WIDTH = BR * BS
F32 = jnp.float32
BF16 = jnp.bfloat16
DIRS = (
    (1, 0, 0, 1, 0),
    (0, 0, 1, 1, 1),
    (-1, 0, 0, 3, 0),
    (0, 0, -1, 3, 1),
    (0, 1, 0, 2, 0),
    (0, -1, 0, 2, 1),
)


def fit(slopes, w, r, place):
    wl = [s * w for s in slopes]
    gamma = [[None] * 5 for _ in range(5)]
    for a in range(5):
        for b in range(a + 1):
            gamma[a][b] = jnp.sum(wl[a] * slopes[b], axis=0, keepdims=True) + (1.0 if a == b else 0.0)
    beta = [jnp.sum(wl[a] * r, axis=0, keepdims=True) for a in range(5)]
    factor = [[None] * 5 for _ in range(5)]
    inverse = [None] * 5
    for j in range(5):
        center = gamma[j][j]
        for k in range(j):
            center = center - factor[j][k] * factor[j][k]
        factor[j][j] = jnp.sqrt(center)
        inverse[j] = 1.0 / factor[j][j]
        for i in range(j + 1, 5):
            off = gamma[i][j]
            for k in range(j):
                off = off - factor[i][k] * factor[j][k]
            factor[i][j] = off * inverse[j]
    solved, target = [], []
    for j in range(5):
        cur, tgt = wl[j], beta[j]
        for k in range(j):
            cur = cur - factor[j][k] * solved[k]
            tgt = tgt - factor[j][k] * target[k]
        solved.append(cur * inverse[j])
        target.append(tgt * inverse[j])
    hit = w * r
    for k in range(5):
        hit = hit - solved[k] * target[k]
    full = jnp.concatenate(solved + [hit, w, place], axis=0)
    return jnp.transpose(full).astype(BF16)


def kernel(
    place_ref, g_ref, slope_ref, weight_ref, resid_ref, block_ref, count_ref, region_ref,
    out_ref, vec_ref, idx_ref, idx_vec,
    gsend, grecv, asend, arecv, fitted, lhs, s_buf, d_acc, v_acc, psend, precv, vrecv,
    gs_sem, gr_sem, as_sem, ar_sem, ps_sem, pr_sem, vs_sem, vr_sem, idx_sem,
):
    region = lax.axis_index("region")
    tile = lax.axis_index("tile")
    z, core = region // 2, region % 2
    y, x = tile // 4, tile % 4
    colour = (x + 2 * y + z) % 4

    def device(nx, ny, nz, ncore):
        return {"region": nz * 2 + ncore, "tile": ny * 4 + nx}

    def neighbour(d, ncore):
        dx, dy, dz = DIRS[d][:3]
        return device((x + dx + 4) % 4, (y + dy + 4) % 4, (z + dz + 4) % 4, ncore)

    sibling = device(x, y, z, 1 - core)

    barrier = pltpu.get_barrier_semaphore()
    for d in range(6):
        for c in range(2):
            pl.semaphore_signal(barrier, inc=1, device_id=neighbour(d, c))
    pl.semaphore_signal(barrier, inc=1, device_id=sibling)

    def worker_of(i, rz):
        wy, wx = i // 4, i % 4
        return {"region": ((rz - wx - 2 * wy + 12) % 4) * 2 + core, "tile": i}

    own_worker = (x + 2 * y) % 4 == 0

    def greet(i, carry):
        @pl.when(jnp.logical_not(jnp.logical_and(own_worker, i == tile)))
        def _():
            pl.semaphore_signal(barrier, inc=1, device_id=worker_of(i, z))
        return carry

    lax.fori_loop(0, 16, greet, 0)
    reg = region_ref[...]
    tracks8 = lax.broadcasted_iota(jnp.int32, (BR, TRK), 0)
    named = jnp.where(reg == tracks8, 1.0, 0.0)
    earlier = (
        lax.broadcasted_iota(jnp.int32, (TRK, TRK), 0) < lax.broadcasted_iota(jnp.int32, (TRK, TRK), 1))
    ahead = jnp.dot(named.astype(BF16), jnp.where(earlier, 1.0, 0.0).astype(BF16), preferred_element_type=F32)
    slot = reg.astype(F32) * CAP + jnp.sum(named * ahead, axis=0, keepdims=True)
    slot_col = jnp.transpose(jnp.broadcast_to(slot, (BR, TRK)))[:, 0:1]
    slot_lane = lax.broadcasted_iota(jnp.int32, (TRK, N_REGION * CAP), 1).astype(F32)
    onehot = jnp.where(slot_col == slot_lane, 1.0, 0.0).astype(BF16)
    number = lax.broadcasted_iota(jnp.int32, (BR, TRK), 1).astype(F32).astype(BF16)
    idx_vec[...] = jnp.dot(number, onehot, preferred_element_type=F32).astype(jnp.int32)
    idx_copy = pltpu.make_async_copy(idx_vec.at[pl.ds(0, 1)], idx_ref, idx_sem)
    idx_copy.start()
    idx_copy.wait()

    def gather(q, ref, k):
        def body(i, carry):
            ref[k, i] = g_ref[jnp.clip(idx_ref[0, q * HALF + i], 0, TRK - 1)]
            return carry
        lax.fori_loop(0, HALF, body, 0, unroll=4)

    def chunk_of(d, c):
        step, half = DIRS[d][3:]
        return (((colour + step) % 4) * 2 + c) * 2 + half

    def g_copy(d, u):
        k = u * 6 + d
        return pltpu.make_async_remote_copy(
            src_ref=gsend.at[k], dst_ref=grecv.at[k],
            send_sem=gs_sem.at[k], recv_sem=gr_sem.at[k],
            device_id=neighbour(d, core ^ u))

    def a_copy(d, u):
        k = u * 6 + d
        return pltpu.make_async_remote_copy(
            src_ref=asend.at[k], dst_ref=arecv.at[k],
            send_sem=as_sem.at[k], recv_sem=ar_sem.at[k],
            device_id=neighbour(d, core ^ u))

    def g_sib(h):
        return pltpu.make_async_remote_copy(
            src_ref=gsend.at[12 + h], dst_ref=grecv.at[12 + 2 * core + h],
            send_sem=gs_sem.at[12 + h], recv_sem=gr_sem.at[12 + 2 * core + h],
            device_id=sibling)

    def a_sib(h):
        return pltpu.make_async_remote_copy(
            src_ref=asend.at[12 + h], dst_ref=arecv.at[12 + 2 * core + h],
            send_sem=as_sem.at[12 + h], recv_sem=ar_sem.at[12 + 2 * core + h],
            device_id=sibling)

    for u in range(2):
        for d in range(6):
            gather(chunk_of(d, core ^ u), gsend, u * 6 + d)
            if u == 0 and d == 0:
                pl.semaphore_wait(barrier, jnp.where(own_worker, 28, 29))
            g_copy(d, u).start()
    for h in range(2):
        gather((colour * 2 + 1 - core) * 2 + h, gsend, 12 + h)
        g_sib(h).start()
    for h in range(2):
        gather((colour * 2 + core) * 2 + h, grecv, 12 + 2 * core + h)

    live = lax.broadcasted_iota(jnp.int32, (HITS, TRK), 0) < count_ref[...]
    weight = jnp.where(live, weight_ref[...].astype(F32), 0.0)
    ids = block_ref[...]
    place = jnp.zeros((HITS, TRK), F32)
    for b in range(BR):
        place = jnp.where(ids == b, place_ref[b].astype(F32), place)
    fitted[...] = fit(
        [slope_ref[c].astype(F32) for c in range(5)], weight, resid_ref[...].astype(F32), place)

    def pick(q):
        rows = (q * HALF + lax.broadcasted_iota(jnp.int32, (HALF, TRK), 0)).astype(F32)
        chosen = jnp.where(slot == rows, 1.0, 0.0).astype(BF16)
        return jnp.dot(chosen, fitted[...], preferred_element_type=F32).astype(BF16)

    for u in range(2):
        for d in range(6):
            asend[u * 6 + d] = pick(chunk_of(d, core ^ u))
            a_copy(d, u).start()
    for h in range(2):
        asend[12 + h] = pick((colour * 2 + 1 - core) * 2 + h)
        a_sib(h).start()
    for h in range(2):
        arecv[12 + 2 * core + h] = pick((colour * 2 + core) * 2 + h)

    d_acc[...] = jnp.zeros_like(d_acc)
    v_acc[...] = jnp.zeros_like(v_acc)

    lane = lax.broadcasted_iota(jnp.int32, (GROUP, 128), 1)
    track = lax.broadcasted_iota(jnp.int32, (GROUP, 128), 0)
    residue = track % 4
    blocks = [(lane // HITS + 4 * v) == track for v in range(2)]
    subf = lax.broadcasted_iota(jnp.int32, (GROUP, 256), 0).astype(F32)

    def chunk(m, carry):
        n = jnp.where(m < 2, 12 + 2 * core + m, jnp.where(m < 4, 12 + 2 * (1 - core) + m - 2, m - 4))

        @pl.when(m >= 2)
        def _():
            pltpu.make_async_remote_copy(
                src_ref=gsend.at[0], dst_ref=grecv.at[n], send_sem=gs_sem.at[0],
                recv_sem=gr_sem.at[n], device_id=sibling).wait_recv()
            pltpu.make_async_remote_copy(
                src_ref=asend.at[0], dst_ref=arecv.at[n], send_sem=as_sem.at[0],
                recv_sem=ar_sem.at[n], device_id=sibling).wait_recv()

        a = arecv[n].astype(F32)
        g = grecv[n].reshape(HALF * HITS, BS)
        gt = jnp.transpose(g)
        parts, wps = [], []
        vec = None
        for j in range(3):
            aj = a[GROUP * j : GROUP * j + GROUP]

            turned = []
            for v in range(2):
                half = aj[:, 128 * v : 128 * v + 128]
                turned.append([half] + [pltpu.roll(half, HITS * k, 1) for k in range(1, 4)])

            def spread_lanes(q):
                options = turned[q // 4]
                own_turn = options[(3 - q) % 4]
                for k in range(3):
                    own_turn = jnp.where(residue == k, options[(k - q) % 4], own_turn)
                return jnp.concatenate([jnp.where(b, own_turn, 0.0) for b in blocks], axis=1)

            place = spread_lanes(7)
            base = [spread_lanes(q) for q in range(5)]
            rows = []
            for p in range(BR):
                here = place == float(p)
                rows.extend(jnp.where(here, b, 0.0) for b in base)
            left = jnp.concatenate(rows, axis=0).astype(BF16)
            gj = g[256 * j : 256 * j + 256]
            parts.append(jnp.dot(left, gj, preferred_element_type=F32))
            prow = jnp.sum(place, axis=0, keepdims=True)
            hrow = jnp.sum(spread_lanes(5), axis=0, keepdims=True)
            wrow = jnp.sum(spread_lanes(6), axis=0, keepdims=True)
            onp = subf == prow
            vj = jnp.dot(jnp.where(onp, hrow, 0.0).astype(BF16), gj, preferred_element_type=F32)
            vec = vj if vec is None else vec + vj
            wps.append(jnp.where(onp, wrow, 0.0).astype(BF16))
        v_acc[...] += vec
        wp = jnp.concatenate(wps, axis=1)
        pad = jnp.zeros((8, BS), F32)
        for p in range(BR):
            piece = jnp.concatenate([q[40 * p : 40 * p + 40] for q in parts] + [pad], axis=0)
            s_buf[pl.ds(pl.multiple_of(m * 128, 128), 128), BS * p : BS * p + BS] = piece.astype(BF16)
            lhs[BS * p : BS * p + BS, :] = gt * wp[p : p + 1, :]
        d_acc[...] += jnp.dot(lhs[...], g, preferred_element_type=F32)
        return carry

    lax.fori_loop(0, CHUNKS, chunk, 0)

    def p_copy(i):
        return pltpu.make_async_remote_copy(
            src_ref=psend.at[i], dst_ref=precv.at[tile],
            send_sem=ps_sem.at[i], recv_sem=pr_sem.at[tile],
            device_id={"region": colour * 2 + core, "tile": i})

    def v_copy(i):
        return pltpu.make_async_remote_copy(
            src_ref=v_acc, dst_ref=vrecv.at[tile],
            send_sem=vs_sem.at[i], recv_sem=vr_sem.at[tile],
            device_id={"region": colour * 2 + core, "tile": i})

    def is_self(i):
        return jnp.logical_and(own_worker, i == tile)

    def piece(s, carry):
        a = (y + s) % 4
        cols = pl.ds(pl.multiple_of(a * 256, 256), 256)
        prod = lax.dot_general(
            s_buf[:, cols], s_buf[...], (((0,), (0,)), ((), ())), preferred_element_type=F32)
        lhs_cols = lax.broadcasted_iota(jnp.int32, (1, WIDTH), 1) // BS
        for e in range(2):
            dblock = d_acc[pl.ds(pl.multiple_of(a * 256 + e * 128, 128), 128), :]
            wide = jnp.concatenate([dblock] * BR, axis=1)
            part = jnp.where(lhs_cols == a * 2 + e, wide, 0.0) - prod[e * 128 : e * 128 + 128]
            part = part.astype(BF16)
            for u in range(2):
                psend[a * 4 + e * 2 + u] = part[ROWS * u : ROWS * u + ROWS]
        for u in range(4):
            i = a * 4 + (x + u) % 4

            @pl.when(jnp.logical_not(is_self(i)))
            def _():
                p_copy(i).start()
                v_copy(i).start()

            @pl.when(is_self(i))
            def _():
                precv[tile] = psend[i]
                vrecv[tile] = v_acc[...]
        return carry

    lax.fori_loop(0, 4, piece, 0)

    def collect(i, carry):
        @pl.when(jnp.logical_not(is_self(i)))
        def _():
            pltpu.make_async_remote_copy(
                src_ref=psend.at[0], dst_ref=precv.at[i], send_sem=ps_sem.at[0],
                recv_sem=pr_sem.at[i], device_id=sibling).wait_recv()
            pltpu.make_async_remote_copy(
                src_ref=v_acc, dst_ref=vrecv.at[i], send_sem=vs_sem.at[0],
                recv_sem=vr_sem.at[i], device_id=sibling).wait_recv()
        return carry

    lax.fori_loop(0, 16, collect, 0)

    total = precv[0].astype(F32)
    vtot = vrecv[0]
    for i in range(1, 16):
        total = total + precv[i].astype(F32)
        vtot = vtot + vrecv[i]
    out_ref[0] = total
    mine = lax.broadcasted_iota(jnp.int32, (BR, BS), 0) == tile // 2
    row = jnp.sum(jnp.where(mine, vtot, 0.0), axis=0, keepdims=True)
    vec_ref[...] = jnp.where(tile % 2 == 0, row[:, :ROWS], row[:, ROWS:])

    for u in range(2):
        for d in range(6):
            g_copy(d, u).wait_send()
            a_copy(d, u).wait_send()
    for h in range(2):
        g_sib(h).wait_send()
        a_sib(h).wait_send()

    def finish(i, carry):
        @pl.when(jnp.logical_not(is_self(i)))
        def _():
            p_copy(i).wait_send()
            v_copy(i).wait_send()
        return carry

    lax.fori_loop(0, 16, finish, 0)


def local(
    global_deriv,
    local_deriv,
    hit_weight,
    hit_resid,
    block_ids,
    hit_count,
    track_region,
    block_place,
):
    vmem = pl.BlockSpec(memory_space=pltpu.VMEM)
    dma = pltpu.SemaphoreType.DMA
    return pl.pallas_call(
        kernel,
        name="assemble",
        out_shape=(
            jax.ShapeDtypeStruct((1, ROWS, WIDTH), F32),
            jax.ShapeDtypeStruct((1, ROWS), F32),
        ),
        in_specs=[pl.BlockSpec(memory_space=pltpu.SMEM)] + [vmem] * 7,
        out_specs=(vmem, vmem),
        scratch_shapes=[
            pltpu.SMEM((1, N_REGION * CAP), jnp.int32),
            pltpu.VMEM((BR, N_REGION * CAP), jnp.int32),
            pltpu.VMEM((14, HALF, HITS, BS), BF16),
            pltpu.VMEM((CHUNKS, HALF, HITS, BS), BF16),
            pltpu.VMEM((14, HALF, 256), BF16),
            pltpu.VMEM((CHUNKS, HALF, 256), BF16),
            pltpu.VMEM((TRK, 256), BF16),
            pltpu.VMEM((WIDTH, HALF * HITS), BF16),
            pltpu.VMEM((CHUNKS * 128, WIDTH), BF16),
            pltpu.VMEM((WIDTH, BS), F32),
            pltpu.VMEM((BR, BS), F32),
            pltpu.VMEM((16, ROWS, WIDTH), BF16),
            pltpu.VMEM((16, ROWS, WIDTH), BF16),
            pltpu.VMEM((16, BR, BS), F32),
            dma((14,)), dma((16,)), dma((14,)), dma((16,)),
            dma((16,)), dma((16,)), dma((16,)), dma((16,)), dma,
        ],
        compiler_params=pltpu.CompilerParams(
            collective_id=0, has_side_effects=True, vmem_limit_bytes=56 << 20),
    )(
        block_place, global_deriv, local_deriv.transpose(1, 2, 0), hit_weight.T, hit_resid.T,
        block_ids.T, hit_count.reshape(1, TRK), track_region.reshape(1, TRK))


def solution(mesh):
    return jax.shard_map(
        local,
        mesh=mesh,
        in_specs=(
            P(("region", "tile"), None, None),
            P(("region", "tile"), None, None),
            P(("region", "tile"), None),
            P(("region", "tile"), None),
            P(("region", "tile"), None),
            P(("region", "tile")),
            P(("region", "tile"), None),
            P(),
        ),
        out_specs=(P("region", "tile", None), P("region", "tile")),
        check_vma=False,
    )
```

```python
import functools

import jax
import jax.numpy as jnp
from jax import lax
from jax.experimental import pallas as pl
from jax.experimental.pallas import tpu as pltpu
from jax.sharding import PartitionSpec as P

BS = 128
BR = 8
HITS = 32
TRK = 192
CAP = 48
N_REGION = 8
HALF = CAP // 2
GROUP = 8
CHUNKS = 16
ROWS = 64
WIDTH = BR * BS
F32 = jnp.float32
BF16 = jnp.bfloat16
DIRS = (
    (1, 0, 0, 1, 0),
    (0, 0, 1, 1, 1),
    (-1, 0, 0, 3, 0),
    (0, 0, -1, 3, 1),
    (0, 1, 0, 2, 0),
    (0, -1, 0, 2, 1),
)


def fit(slopes, w, r, place):
    wl = [s * w for s in slopes]
    gamma = [[None] * 5 for _ in range(5)]
    for a in range(5):
        for b in range(a + 1):
            gamma[a][b] = jnp.sum(wl[a] * slopes[b], axis=0, keepdims=True) + (1.0 if a == b else 0.0)
    beta = [jnp.sum(wl[a] * r, axis=0, keepdims=True) for a in range(5)]
    factor = [[None] * 5 for _ in range(5)]
    inverse = [None] * 5
    for j in range(5):
        center = gamma[j][j]
        for k in range(j):
            center = center - factor[j][k] * factor[j][k]
        factor[j][j] = jnp.sqrt(center)
        inverse[j] = 1.0 / factor[j][j]
        for i in range(j + 1, 5):
            off = gamma[i][j]
            for k in range(j):
                off = off - factor[i][k] * factor[j][k]
            factor[i][j] = off * inverse[j]
    solved, target = [], []
    for j in range(5):
        cur, tgt = wl[j], beta[j]
        for k in range(j):
            cur = cur - factor[j][k] * solved[k]
            tgt = tgt - factor[j][k] * target[k]
        solved.append(cur * inverse[j])
        target.append(tgt * inverse[j])
    hit = w * r
    for k in range(5):
        hit = hit - solved[k] * target[k]
    full = jnp.concatenate(solved + [hit, w, place], axis=0)
    return jnp.transpose(full).astype(BF16)


def kernel(
    place_ref, g_ref, slope_ref, weight_ref, resid_ref, block_ref, count_ref, region_ref,
    out_ref, vec_ref, idx_ref, idx_vec,
    gsend, grecv, asend, arecv, fitted, lhs, wp_buf, s_buf, d_acc, v_acc,
    psend, precv, vrecv, dsend, drecv, xsend, xrecv,
    gs_sem, gr_sem, as_sem, ar_sem, ps_sem, pr_sem, vs_sem, vr_sem, ds_sem, dr_sem, xs_sem, xr_sem, idx_sem,
):
    region = lax.axis_index("region")
    tile = lax.axis_index("tile")
    z, core = region // 2, region % 2
    y, x = tile // 4, tile % 4
    colour = (x + 2 * y + z) % 4

    def device(nx, ny, nz, ncore):
        return {"region": nz * 2 + ncore, "tile": ny * 4 + nx}

    def neighbour(d, ncore):
        dx, dy, dz = DIRS[d][:3]
        return device((x + dx + 4) % 4, (y + dy + 4) % 4, (z + dz + 4) % 4, ncore)

    sibling = device(x, y, z, 1 - core)

    barrier = pltpu.get_barrier_semaphore()
    for d in range(6):
        for c in range(2):
            pl.semaphore_signal(barrier, inc=1, device_id=neighbour(d, c))
    pl.semaphore_signal(barrier, inc=1, device_id=sibling)

    def worker_of(i, rz):
        wy, wx = i // 4, i % 4
        return {"region": ((rz - wx - 2 * wy + 12) % 4) * 2 + core, "tile": i}

    own_worker = (x + 2 * y) % 4 == 0

    def greet(i, carry):
        @pl.when(jnp.logical_not(jnp.logical_and(own_worker, i == tile)))
        def _():
            pl.semaphore_signal(barrier, inc=1, device_id=worker_of(i, z))
        return carry

    lax.fori_loop(0, 16, greet, 0)
    mine = tile // 2

    def owner(a, e):
        return {"region": region, "tile": ((a + 8) % 8) * 2 + e}

    for j in range(1, 4):
        for e in range(2):
            pl.semaphore_signal(barrier, inc=1, device_id=owner(mine - j, e))

    @pl.when(mine >= 4)
    def _():
        for e in range(2):
            pl.semaphore_signal(barrier, inc=1, device_id=owner(mine - 4, e))

    reg = region_ref[...]
    tracks8 = lax.broadcasted_iota(jnp.int32, (BR, TRK), 0)
    named = jnp.where(reg == tracks8, 1.0, 0.0)
    earlier = (
        lax.broadcasted_iota(jnp.int32, (TRK, TRK), 0) < lax.broadcasted_iota(jnp.int32, (TRK, TRK), 1))
    ahead = jnp.dot(named.astype(BF16), jnp.where(earlier, 1.0, 0.0).astype(BF16), preferred_element_type=F32)
    slot = reg.astype(F32) * CAP + jnp.sum(named * ahead, axis=0, keepdims=True)
    slot_col = jnp.transpose(jnp.broadcast_to(slot, (BR, TRK)))[:, 0:1]
    slot_lane = lax.broadcasted_iota(jnp.int32, (TRK, N_REGION * CAP), 1).astype(F32)
    onehot = jnp.where(slot_col == slot_lane, 1.0, 0.0).astype(BF16)
    number = lax.broadcasted_iota(jnp.int32, (BR, TRK), 1).astype(F32).astype(BF16)
    idx_vec[...] = jnp.dot(number, onehot, preferred_element_type=F32).astype(jnp.int32)
    idx_copy = pltpu.make_async_copy(idx_vec.at[pl.ds(0, 1)], idx_ref, idx_sem)
    idx_copy.start()
    idx_copy.wait()

    def gather(q, ref, k):
        def body(i, carry):
            ref[k, i] = g_ref[jnp.clip(idx_ref[0, q * HALF + i], 0, TRK - 1)]
            return carry
        lax.fori_loop(0, HALF, body, 0, unroll=4)

    def chunk_of(d, c):
        step, half = DIRS[d][3:]
        return (((colour + step) % 4) * 2 + c) * 2 + half

    def g_copy(d, u):
        k = u * 6 + d
        return pltpu.make_async_remote_copy(
            src_ref=gsend.at[k], dst_ref=grecv.at[k],
            send_sem=gs_sem.at[k], recv_sem=gr_sem.at[k],
            device_id=neighbour(d, core ^ u))

    def a_copy(d, u):
        k = u * 6 + d
        return pltpu.make_async_remote_copy(
            src_ref=asend.at[k], dst_ref=arecv.at[k],
            send_sem=as_sem.at[k], recv_sem=ar_sem.at[k],
            device_id=neighbour(d, core ^ u))

    def g_sib(h):
        return pltpu.make_async_remote_copy(
            src_ref=gsend.at[12 + h], dst_ref=grecv.at[12 + 2 * core + h],
            send_sem=gs_sem.at[12 + h], recv_sem=gr_sem.at[12 + 2 * core + h],
            device_id=sibling)

    def a_sib(h):
        return pltpu.make_async_remote_copy(
            src_ref=asend.at[12 + h], dst_ref=arecv.at[12 + 2 * core + h],
            send_sem=as_sem.at[12 + h], recv_sem=ar_sem.at[12 + 2 * core + h],
            device_id=sibling)

    def send_tracks(u):
        for d in range(6):
            gather(chunk_of(d, core ^ u), gsend, u * 6 + d)
            if u == 0 and d == 0:
                pl.semaphore_wait(
                    barrier, jnp.where(own_worker, 34, 35) + jnp.where(mine < 4, 2, 0))
            g_copy(d, u).start()

    send_tracks(0)

    live = lax.broadcasted_iota(jnp.int32, (HITS, TRK), 0) < count_ref[...]
    weight = jnp.where(live, weight_ref[...].astype(F32), 0.0)
    ids = block_ref[...]
    place = jnp.zeros((HITS, TRK), F32)
    for b in range(BR):
        place = jnp.where(ids == b, place_ref[b].astype(F32), place)
    fitted[...] = fit(
        [slope_ref[c].astype(F32) for c in range(5)], weight, resid_ref[...].astype(F32), place)

    def pick(q):
        rows = (q * HALF + lax.broadcasted_iota(jnp.int32, (HALF, TRK), 0)).astype(F32)
        chosen = jnp.where(slot == rows, 1.0, 0.0).astype(BF16)
        return jnp.dot(chosen, fitted[...], preferred_element_type=F32).astype(BF16)

    for u in range(2):
        for d in range(6):
            asend[u * 6 + d] = pick(chunk_of(d, core ^ u))
            a_copy(d, u).start()
    for h in range(2):
        asend[12 + h] = pick((colour * 2 + 1 - core) * 2 + h)
        a_sib(h).start()
    send_tracks(1)
    for h in range(2):
        gather((colour * 2 + 1 - core) * 2 + h, gsend, 12 + h)
        g_sib(h).start()
    for h in range(2):
        arecv[12 + 2 * core + h] = pick((colour * 2 + core) * 2 + h)
        gather((colour * 2 + core) * 2 + h, grecv, 12 + 2 * core + h)

    v_acc[...] = jnp.zeros_like(v_acc)

    lane = lax.broadcasted_iota(jnp.int32, (GROUP, 128), 1)
    track = lax.broadcasted_iota(jnp.int32, (GROUP, 128), 0)
    residue = track % 4
    blocks = [(lane // HITS + 4 * v) == track for v in range(2)]
    subf = lax.broadcasted_iota(jnp.int32, (GROUP, 256), 0).astype(F32)

    def chunk_at(m):
        return jnp.where(m < 2, 12 + 2 * core + m, jnp.where(m < 4, 12 + 2 * (1 - core) + m - 2, m - 4))

    def chunk(m, carry):
        n = chunk_at(m)

        @pl.when(m >= 2)
        def _():
            pltpu.make_async_remote_copy(
                src_ref=gsend.at[0], dst_ref=grecv.at[n], send_sem=gs_sem.at[0],
                recv_sem=gr_sem.at[n], device_id=sibling).wait_recv()
            pltpu.make_async_remote_copy(
                src_ref=asend.at[0], dst_ref=arecv.at[n], send_sem=as_sem.at[0],
                recv_sem=ar_sem.at[n], device_id=sibling).wait_recv()

        a = arecv[n].astype(F32)
        g = grecv[n].reshape(HALF * HITS, BS)
        parts, wps = [], []
        vec = None
        for j in range(3):
            aj = a[GROUP * j : GROUP * j + GROUP]

            turned = []
            for v in range(2):
                half = aj[:, 128 * v : 128 * v + 128]
                turned.append([half] + [pltpu.roll(half, HITS * k, 1) for k in range(1, 4)])

            def spread_lanes(q):
                options = turned[q // 4]
                own_turn = options[(3 - q) % 4]
                for k in range(3):
                    own_turn = jnp.where(residue == k, options[(k - q) % 4], own_turn)
                return jnp.concatenate([jnp.where(b, own_turn, 0.0) for b in blocks], axis=1)

            place = spread_lanes(7)
            base = [spread_lanes(q) for q in range(5)]
            rows = []
            for p in range(BR):
                here = place == float(p)
                rows.extend(jnp.where(here, b, 0.0) for b in base)
            left = jnp.concatenate(rows, axis=0).astype(BF16)
            gj = g[256 * j : 256 * j + 256]
            parts.append(jnp.dot(left, gj, preferred_element_type=F32))
            prow = jnp.sum(place, axis=0, keepdims=True)
            hrow = jnp.sum(spread_lanes(5), axis=0, keepdims=True)
            wrow = jnp.sum(spread_lanes(6), axis=0, keepdims=True)
            onp = subf == prow
            vj = jnp.dot(jnp.where(onp, hrow, 0.0).astype(BF16), gj, preferred_element_type=F32)
            vec = vj if vec is None else vec + vj
            wps.append(jnp.where(onp, wrow, 0.0).astype(BF16))
        v_acc[...] += vec
        wp_buf[m] = jnp.concatenate(wps, axis=1)
        pad = jnp.zeros((8, BS), F32)
        rows = pl.ds(pl.multiple_of(m * 128, 128), 128)
        for p in range(BR):
            piece = jnp.concatenate([q[40 * p : 40 * p + 40] for q in parts] + [pad], axis=0).astype(BF16)
            s_buf[rows, BS * p : BS * p + BS] = piece
            if p < 4:
                s_buf[rows, WIDTH + BS * p : WIDTH + BS * p + BS] = piece
        return carry

    lax.fori_loop(0, CHUNKS, chunk, 0)

    def target(i):
        return {"region": colour * 2 + core, "tile": i}

    def p_copy(i, count):
        return pltpu.make_async_remote_copy(
            src_ref=psend.at[i, pl.ds(0, count)], dst_ref=precv.at[tile, pl.ds(0, count)],
            send_sem=ps_sem.at[i], recv_sem=pr_sem.at[tile], device_id=target(i))

    def v_copy(i):
        return pltpu.make_async_remote_copy(
            src_ref=v_acc, dst_ref=vrecv.at[tile],
            send_sem=vs_sem.at[i], recv_sem=vr_sem.at[tile], device_id=target(i))

    def d_copy(i):
        return pltpu.make_async_remote_copy(
            src_ref=dsend.at[i], dst_ref=drecv.at[tile],
            send_sem=ds_sem.at[i], recv_sem=dr_sem.at[tile], device_id=target(i))

    def is_self(i):
        return jnp.logical_and(own_worker, i == tile)

    def piece(s, carry):
        yy = (y + s) % 4
        cols = pl.ds(pl.multiple_of(yy * 256, 256), 256)
        wide = pl.ds(pl.multiple_of(yy * 256, 256), 768)
        prod = lax.dot_general(
            s_buf[:, cols], s_buf[:, wide], (((0,), (0,)), ((), ())), preferred_element_type=F32)
        for e in range(2):
            part = -prod[128 * e : 128 * e + 128, 128 * e : 128 * e + 640]
            d_acc[pl.ds(pl.multiple_of(yy * 256 + 128 * e, 128), 128), :] = part[:, :128]
            part = part.astype(BF16)
            for u in range(2):
                for j in range(4):
                    psend[yy * 4 + e * 2 + u, j] = part[ROWS * u : ROWS * u + ROWS, BS * (j + 1) : BS * (j + 2)]
        for u in range(4):
            i = yy * 4 + (x + u) % 4
            other = jnp.logical_not(is_self(i))

            @pl.when(jnp.logical_and(other, yy < 2))
            def _():
                p_copy(i, 4).start()

            @pl.when(jnp.logical_and(other, yy >= 2))
            def _():
                p_copy(i, 3).start()

            @pl.when(other)
            def _():
                v_copy(i).start()

            @pl.when(is_self(i))
            def _():
                precv[tile] = psend[i]
                vrecv[tile] = v_acc[...]
        return carry

    lax.fori_loop(0, 4, piece, 0)

    def diagonal(m, carry):
        g = grecv[chunk_at(m)].reshape(HALF * HITS, BS)
        gt = jnp.transpose(g)
        wp = wp_buf[m]
        for p in range(BR):
            lhs[BS * p : BS * p + BS, :] = gt * wp[p : p + 1, :]
        d_acc[...] += jnp.dot(lhs[...], g, preferred_element_type=F32)
        return carry

    lax.fori_loop(0, CHUNKS, diagonal, 0)

    def send_diagonal(s, carry):
        yy = (y + s // 4) % 4
        i = yy * 4 + (x + s) % 4
        dsend[i] = d_acc[pl.ds(pl.multiple_of(i * ROWS, ROWS), ROWS), :].astype(BF16)

        @pl.when(jnp.logical_not(is_self(i)))
        def _():
            d_copy(i).start()

        @pl.when(is_self(i))
        def _():
            drecv[tile] = dsend[i]
        return carry

    lax.fori_loop(0, 16, send_diagonal, 0)

    def p_arrival(i, count):
        return pltpu.make_async_remote_copy(
            src_ref=psend.at[0, pl.ds(0, count)], dst_ref=precv.at[i, pl.ds(0, count)],
            send_sem=ps_sem.at[0], recv_sem=pr_sem.at[i], device_id=sibling)

    def collect(i, carry):
        other = jnp.logical_not(is_self(i))

        @pl.when(jnp.logical_and(other, mine < 4))
        def _():
            p_arrival(i, 4).wait_recv()

        @pl.when(jnp.logical_and(other, mine >= 4))
        def _():
            p_arrival(i, 3).wait_recv()

        @pl.when(other)
        def _():
            pltpu.make_async_remote_copy(
                src_ref=v_acc, dst_ref=vrecv.at[i], send_sem=vs_sem.at[0],
                recv_sem=vr_sem.at[i], device_id=sibling).wait_recv()
        return carry

    lax.fori_loop(0, 16, collect, 0)

    def x_copy(j, e):
        k = 2 * j - 2 + e
        return pltpu.make_async_remote_copy(
            src_ref=xsend.at[k], dst_ref=xrecv.at[2 * j - 2 + tile % 2],
            send_sem=xs_sem.at[k], recv_sem=xr_sem.at[2 * j - 2 + tile % 2], device_id=owner(mine + j, e))

    def x_arrival(j, e):
        k = 2 * j - 2 + e
        return pltpu.make_async_remote_copy(
            src_ref=xsend.at[k], dst_ref=xrecv.at[k],
            send_sem=xs_sem.at[k], recv_sem=xr_sem.at[k], device_id=sibling)

    def column(b):
        return pl.ds(pl.multiple_of(((b + 8) % 8) * BS, BS), BS)

    def reduce_block(j):
        total = precv[0, j - 1].astype(F32)
        for i in range(1, 16):
            total = total + precv[i, j - 1].astype(F32)
        out_ref[0, :, column(mine + j)] = total
        turned = jnp.transpose(total)
        for e in range(2):
            t = turned[ROWS * e : ROWS * e + ROWS]
            xsend[2 * j - 2 + e] = jnp.concatenate([t[:32], t[32:]], axis=1)
            x_copy(j, e).start()

    def receive_block(j):
        for e in range(2):
            x_arrival(j, e).wait_recv()
        q0, q1 = xrecv[2 * j - 2], xrecv[2 * j - 1]
        out_ref[0, 0:32, column(mine - j)] = jnp.concatenate([q0[:, :ROWS], q1[:, :ROWS]], axis=1)
        out_ref[0, 32:64, column(mine - j)] = jnp.concatenate([q0[:, ROWS:], q1[:, ROWS:]], axis=1)

    @pl.when(mine < 4)
    def _():
        reduce_block(4)

    for j in range(3, 0, -1):
        reduce_block(j)

    vtot = vrecv[0]
    for i in range(1, 16):
        vtot = vtot + vrecv[i]
    here = lax.broadcasted_iota(jnp.int32, (BR, BS), 0) == mine
    row = jnp.sum(jnp.where(here, vtot, 0.0), axis=0, keepdims=True)
    vec_ref[...] = jnp.where(tile % 2 == 0, row[:, :ROWS], row[:, ROWS:])

    def collect_diagonal(i, carry):
        @pl.when(jnp.logical_not(is_self(i)))
        def _():
            pltpu.make_async_remote_copy(
                src_ref=dsend.at[0], dst_ref=drecv.at[i], send_sem=ds_sem.at[0],
                recv_sem=dr_sem.at[i], device_id=sibling).wait_recv()
        return carry

    lax.fori_loop(0, 16, collect_diagonal, 0)
    total = drecv[0].astype(F32)
    for i in range(1, 16):
        total = total + drecv[i].astype(F32)
    out_ref[0, :, column(mine)] = total

    for j in range(1, 4):
        receive_block(j)

    @pl.when(mine >= 4)
    def _():
        receive_block(4)

    for j in range(1, 4):
        for e in range(2):
            x_copy(j, e).wait_send()

    @pl.when(mine < 4)
    def _():
        for e in range(2):
            x_copy(4, e).wait_send()

    for u in range(2):
        for d in range(6):
            g_copy(d, u).wait_send()
            a_copy(d, u).wait_send()
    for h in range(2):
        g_sib(h).wait_send()
        a_sib(h).wait_send()

    def finish(i, carry):
        other = jnp.logical_not(is_self(i))

        @pl.when(jnp.logical_and(other, i < 8))
        def _():
            p_copy(i, 4).wait_send()

        @pl.when(jnp.logical_and(other, i >= 8))
        def _():
            p_copy(i, 3).wait_send()

        @pl.when(other)
        def _():
            v_copy(i).wait_send()
            d_copy(i).wait_send()
        return carry

    lax.fori_loop(0, 16, finish, 0)


def local(
    global_deriv,
    local_deriv,
    hit_weight,
    hit_resid,
    block_ids,
    hit_count,
    track_region,
    block_place,
):
    vmem = pl.BlockSpec(memory_space=pltpu.VMEM)
    dma = pltpu.SemaphoreType.DMA
    return pl.pallas_call(
        kernel,
        name="assemble",
        out_shape=(
            jax.ShapeDtypeStruct((1, ROWS, WIDTH), F32),
            jax.ShapeDtypeStruct((1, ROWS), F32),
        ),
        in_specs=[pl.BlockSpec(memory_space=pltpu.SMEM)] + [vmem] * 7,
        out_specs=(vmem, vmem),
        scratch_shapes=[
            pltpu.SMEM((1, N_REGION * CAP), jnp.int32),
            pltpu.VMEM((BR, N_REGION * CAP), jnp.int32),
            pltpu.VMEM((14, HALF, HITS, BS), BF16),
            pltpu.VMEM((CHUNKS, HALF, HITS, BS), BF16),
            pltpu.VMEM((14, HALF, 256), BF16),
            pltpu.VMEM((CHUNKS, HALF, 256), BF16),
            pltpu.VMEM((TRK, 256), BF16),
            pltpu.VMEM((WIDTH, HALF * HITS), BF16),
            pltpu.VMEM((CHUNKS, BR, HALF * HITS), BF16),
            pltpu.VMEM((CHUNKS * 128, WIDTH + WIDTH // 2), BF16),
            pltpu.VMEM((WIDTH, BS), F32),
            pltpu.VMEM((BR, BS), F32),
            pltpu.VMEM((16, 4, ROWS, BS), BF16),
            pltpu.VMEM((16, 4, ROWS, BS), BF16),
            pltpu.VMEM((16, BR, BS), F32),
            pltpu.VMEM((16, ROWS, BS), BF16),
            pltpu.VMEM((16, ROWS, BS), BF16),
            pltpu.VMEM((8, 32, BS), F32),
            pltpu.VMEM((8, 32, BS), F32),
            dma((14,)), dma((16,)), dma((14,)), dma((16,)),
            dma((16,)), dma((16,)), dma((16,)), dma((16,)), dma((16,)), dma((16,)), dma((8,)), dma((8,)), dma,
        ],
        compiler_params=pltpu.CompilerParams(
            collective_id=0, has_side_effects=True, vmem_limit_bytes=56 << 20),
    )(
        block_place, global_deriv, local_deriv.transpose(1, 2, 0), hit_weight.T, hit_resid.T,
        block_ids.T, hit_count.reshape(1, TRK), track_region.reshape(1, TRK))


def solution(mesh):
    return jax.shard_map(
        local,
        mesh=mesh,
        in_specs=(
            P(("region", "tile"), None, None),
            P(("region", "tile"), None, None),
            P(("region", "tile"), None),
            P(("region", "tile"), None),
            P(("region", "tile"), None),
            P(("region", "tile")),
            P(("region", "tile"), None),
            P(),
        ),
        out_specs=(P("region", "tile", None), P("region", "tile")),
        check_vma=False,
    )
```

```python
import functools

import jax
import jax.numpy as jnp
from jax import lax
from jax.experimental import pallas as pl
from jax.experimental.pallas import tpu as pltpu
from jax.sharding import PartitionSpec as P

BS = 128
BR = 8
HITS = 32
TRK = 192
CAP = 48
N_REGION = 8
HALF = CAP // 2
GROUP = 8
CHUNKS = 16
ROWS = 64
WIDTH = BR * BS
F32 = jnp.float32
BF16 = jnp.bfloat16
DIRS = (
    (1, 0, 0, 1, 0),
    (0, 0, 1, 1, 1),
    (-1, 0, 0, 3, 0),
    (0, 0, -1, 3, 1),
    (0, 1, 0, 2, 0),
    (0, -1, 0, 2, 1),
)


def fit(slopes, w, r, place):
    wl = [s * w for s in slopes]
    gamma = [[None] * 5 for _ in range(5)]
    for a in range(5):
        for b in range(a + 1):
            gamma[a][b] = jnp.sum(wl[a] * slopes[b], axis=0, keepdims=True) + (1.0 if a == b else 0.0)
    beta = [jnp.sum(wl[a] * r, axis=0, keepdims=True) for a in range(5)]
    factor = [[None] * 5 for _ in range(5)]
    inverse = [None] * 5
    for j in range(5):
        center = gamma[j][j]
        for k in range(j):
            center = center - factor[j][k] * factor[j][k]
        factor[j][j] = jnp.sqrt(center)
        inverse[j] = 1.0 / factor[j][j]
        for i in range(j + 1, 5):
            off = gamma[i][j]
            for k in range(j):
                off = off - factor[i][k] * factor[j][k]
            factor[i][j] = off * inverse[j]
    solved, target = [], []
    for j in range(5):
        cur, tgt = wl[j], beta[j]
        for k in range(j):
            cur = cur - factor[j][k] * solved[k]
            tgt = tgt - factor[j][k] * target[k]
        solved.append(cur * inverse[j])
        target.append(tgt * inverse[j])
    hit = w * r
    for k in range(5):
        hit = hit - solved[k] * target[k]
    full = jnp.concatenate(solved + [hit, w, place], axis=0)
    return jnp.transpose(full).astype(BF16)


def kernel(
    place_ref, g_ref, slope_ref, weight_ref, resid_ref, block_ref, count_ref, region_ref,
    out_ref, vec_ref, idx_ref, idx_vec,
    gsend, grecv, asend, arecv, fitted, lhs, wp_buf, s_buf, p_acc, d_acc, v_acc, vsend,
    psend, precv, vrecv, dsend, drecv, xsend, xrecv,
    gs_sem, gr_sem, as_sem, ar_sem, ps_sem, pr_sem, vs_sem, vr_sem, ds_sem, dr_sem, xs_sem, xr_sem, idx_sem,
):
    region = lax.axis_index("region")
    tile = lax.axis_index("tile")
    z, core = region // 2, region % 2
    y, x = tile // 4, tile % 4
    colour = (x + 2 * y + z) % 4

    def device(nx, ny, nz, ncore):
        return {"region": nz * 2 + ncore, "tile": ny * 4 + nx}

    def neighbour(d, ncore):
        dx, dy, dz = DIRS[d][:3]
        return device((x + dx + 4) % 4, (y + dy + 4) % 4, (z + dz + 4) % 4, ncore)

    sibling = device(x, y, z, 1 - core)

    barrier = pltpu.get_barrier_semaphore()
    for d in range(6):
        for c in range(2):
            pl.semaphore_signal(barrier, inc=1, device_id=neighbour(d, c))
    pl.semaphore_signal(barrier, inc=1, device_id=sibling)

    def worker_of(i, rz):
        wy, wx = i // 4, i % 4
        return {"region": ((rz - wx - 2 * wy + 12) % 4) * 2 + core, "tile": i}

    own_worker = (x + 2 * y) % 4 == 0

    def greet(i, carry):
        @pl.when(jnp.logical_not(jnp.logical_and(own_worker, i == tile)))
        def _():
            pl.semaphore_signal(barrier, inc=1, device_id=worker_of(i, z))
        return carry

    lax.fori_loop(0, 16, greet, 0)
    mine = tile // 2

    def owner(a, e):
        return {"region": region, "tile": ((a + 8) % 8) * 2 + e}

    for j in range(1, 4):
        for e in range(2):
            pl.semaphore_signal(barrier, inc=1, device_id=owner(mine - j, e))

    @pl.when(mine >= 4)
    def _():
        for e in range(2):
            pl.semaphore_signal(barrier, inc=1, device_id=owner(mine - 4, e))

    reg = region_ref[...]
    tracks8 = lax.broadcasted_iota(jnp.int32, (BR, TRK), 0)
    named = jnp.where(reg == tracks8, 1.0, 0.0)
    earlier = (
        lax.broadcasted_iota(jnp.int32, (TRK, TRK), 0) < lax.broadcasted_iota(jnp.int32, (TRK, TRK), 1))
    ahead = jnp.dot(named.astype(BF16), jnp.where(earlier, 1.0, 0.0).astype(BF16), preferred_element_type=F32)
    slot = reg.astype(F32) * CAP + jnp.sum(named * ahead, axis=0, keepdims=True)
    slot_col = jnp.transpose(jnp.broadcast_to(slot, (BR, TRK)))[:, 0:1]
    slot_lane = lax.broadcasted_iota(jnp.int32, (TRK, N_REGION * CAP), 1).astype(F32)
    onehot = jnp.where(slot_col == slot_lane, 1.0, 0.0).astype(BF16)
    number = lax.broadcasted_iota(jnp.int32, (BR, TRK), 1).astype(F32).astype(BF16)
    idx_vec[...] = jnp.dot(number, onehot, preferred_element_type=F32).astype(jnp.int32)
    idx_copy = pltpu.make_async_copy(idx_vec.at[pl.ds(0, 1)], idx_ref, idx_sem)
    idx_copy.start()
    idx_copy.wait()

    def gather(q, t, ref, k):
        for i in range(GROUP):
            ref[k, t, i] = g_ref[jnp.clip(idx_ref[0, q * HALF + t * GROUP + i], 0, TRK - 1)]

    def chunk_of(d, c):
        step, half = DIRS[d][3:]
        return (((colour + step) % 4) * 2 + c) * 2 + half

    def g_copy(d, u, t):
        k = u * 6 + d
        return pltpu.make_async_remote_copy(
            src_ref=gsend.at[k, t], dst_ref=grecv.at[k, t],
            send_sem=gs_sem.at[k, t], recv_sem=gr_sem.at[k, t],
            device_id=neighbour(d, core ^ u))

    def a_copy(d, u):
        k = u * 6 + d
        return pltpu.make_async_remote_copy(
            src_ref=asend.at[k], dst_ref=arecv.at[k],
            send_sem=as_sem.at[k], recv_sem=ar_sem.at[k],
            device_id=neighbour(d, core ^ u))

    def g_sib(h, t):
        return pltpu.make_async_remote_copy(
            src_ref=gsend.at[12 + h, t], dst_ref=grecv.at[12 + 2 * core + h, t],
            send_sem=gs_sem.at[12 + h, t], recv_sem=gr_sem.at[12 + 2 * core + h, t],
            device_id=sibling)

    def a_sib(h):
        return pltpu.make_async_remote_copy(
            src_ref=asend.at[12 + h], dst_ref=arecv.at[12 + 2 * core + h],
            send_sem=as_sem.at[12 + h], recv_sem=ar_sem.at[12 + 2 * core + h],
            device_id=sibling)

    def send_tracks(u):
        for t in range(3):
            for d in range(6):
                gather(chunk_of(d, core ^ u), t, gsend, u * 6 + d)
                if u == 0 and t == 0 and d == 0:
                    pl.semaphore_wait(
                        barrier, jnp.where(own_worker, 34, 35) + jnp.where(mine < 4, 2, 0))
                g_copy(d, u, t).start()

    send_tracks(0)

    live = lax.broadcasted_iota(jnp.int32, (HITS, TRK), 0) < count_ref[...]
    weight = jnp.where(live, weight_ref[...].astype(F32), 0.0)
    ids = block_ref[...]
    place = jnp.zeros((HITS, TRK), F32)
    for b in range(BR):
        place = jnp.where(ids == b, place_ref[b].astype(F32), place)
    fitted[...] = fit(
        [slope_ref[c].astype(F32) for c in range(5)], weight, resid_ref[...].astype(F32), place)

    def pick(q, ref, k):
        rows = (q * HALF + lax.broadcasted_iota(jnp.int32, (HALF, TRK), 0)).astype(F32)
        chosen = jnp.where(slot == rows, 1.0, 0.0).astype(BF16)
        picked = jnp.dot(chosen, fitted[...], preferred_element_type=F32)
        for t in range(3):
            ref[k, t] = picked[GROUP * t : GROUP * t + GROUP].astype(BF16)

    for u in range(2):
        for d in range(6):
            pick(chunk_of(d, core ^ u), asend, u * 6 + d)
            a_copy(d, u).start()
    for h in range(2):
        pick((colour * 2 + 1 - core) * 2 + h, asend, 12 + h)
        a_sib(h).start()
    send_tracks(1)
    for h in range(2):
        for t in range(3):
            gather((colour * 2 + 1 - core) * 2 + h, t, gsend, 12 + h)
            g_sib(h, t).start()
    for h in range(2):
        pick((colour * 2 + core) * 2 + h, arecv, 12 + 2 * core + h)
        for t in range(3):
            gather((colour * 2 + core) * 2 + h, t, grecv, 12 + 2 * core + h)

    v_acc[...] = jnp.zeros_like(v_acc)

    lane = lax.broadcasted_iota(jnp.int32, (GROUP, 128), 1)
    track = lax.broadcasted_iota(jnp.int32, (GROUP, 128), 0)
    residue = track % 4
    blocks = [(lane // HITS + 4 * v) == track for v in range(2)]
    subf = lax.broadcasted_iota(jnp.int32, (GROUP, 256), 0).astype(F32)

    def group_of(m, q):
        far = m - 2
        source = jnp.where(m == 0, core, 1 - core)
        k = jnp.where(m < 2, 12 + 2 * source + q // 3, far // 3 * 6 + q)
        return k, jnp.where(m < 2, q % 3, far % 3)

    def batch(m, carry):
        found = [group_of(m, q) for q in range(6)]

        @pl.when(m >= 1)
        def _():
            for k, t in found:
                pltpu.make_async_remote_copy(
                    src_ref=gsend.at[0, 0], dst_ref=grecv.at[k, t], send_sem=gs_sem.at[0, 0],
                    recv_sem=gr_sem.at[k, t], device_id=sibling).wait_recv()

        def aux_arrival(k):
            pltpu.make_async_remote_copy(
                src_ref=asend.at[0], dst_ref=arecv.at[k], send_sem=as_sem.at[0],
                recv_sem=ar_sem.at[k], device_id=sibling).wait_recv()

        @pl.when(m == 1)
        def _():
            for h in range(2):
                aux_arrival(12 + 2 * (1 - core) + h)

        @pl.when(jnp.logical_and(m >= 2, (m - 2) % 3 == 0))
        def _():
            for d in range(6):
                aux_arrival((m - 2) // 3 * 6 + d)

        parts, wps = [], []
        vec = None
        for k, t in found:
            aj = arecv[k, t].astype(F32)
            gj = grecv[k, t].reshape(GROUP * HITS, BS)
            turned = []
            for v in range(2):
                half = aj[:, 128 * v : 128 * v + 128]
                turned.append([half] + [pltpu.roll(half, HITS * k, 1) for k in range(1, 4)])

            def spread_lanes(q):
                options = turned[q // 4]
                own_turn = options[(3 - q) % 4]
                for k in range(3):
                    own_turn = jnp.where(residue == k, options[(k - q) % 4], own_turn)
                return jnp.concatenate([jnp.where(b, own_turn, 0.0) for b in blocks], axis=1)

            place = spread_lanes(7)
            base = [spread_lanes(q) for q in range(5)]
            rows = []
            for p in range(BR):
                here = place == float(p)
                rows.extend(jnp.where(here, b, 0.0) for b in base)
            left = jnp.concatenate(rows, axis=0).astype(BF16)
            parts.append(jnp.dot(left, gj, preferred_element_type=F32))
            prow = jnp.sum(place, axis=0, keepdims=True)
            hrow = jnp.sum(spread_lanes(5), axis=0, keepdims=True)
            wrow = jnp.sum(spread_lanes(6), axis=0, keepdims=True)
            onp = subf == prow
            vj = jnp.dot(jnp.where(onp, hrow, 0.0).astype(BF16), gj, preferred_element_type=F32)
            vec = vj if vec is None else vec + vj
            wps.append(jnp.where(onp, wrow, 0.0).astype(BF16))
        v_acc[...] += vec
        for h in range(2):
            wp_buf[2 * m + h] = jnp.concatenate(wps[3 * h : 3 * h + 3], axis=1)
        rows = pl.ds(pl.multiple_of(m * 240, 16), 240)
        for p in range(BR):
            piece = jnp.concatenate([q[40 * p : 40 * p + 40] for q in parts], axis=0).astype(BF16)
            s_buf[rows, BS * p : BS * p + BS] = piece
            if p < 4:
                s_buf[rows, WIDTH + BS * p : WIDTH + BS * p + BS] = piece
        return carry

    def product(yy, first, count):
        start = pl.multiple_of(yy * 256, 256)
        return lax.dot_general(
            s_buf[first : first + count, pl.ds(start, 256)], s_buf[first : first + count, pl.ds(start, 768)],
            (((0,), (0,)), ((), ())), preferred_element_type=F32)

    def accumulate(first, count):
        def body(yy, carry):
            p = product(yy, first, count)
            p_acc[yy] = p if first == 0 else p_acc[yy] + p
            return carry
        lax.fori_loop(0, 4, body, 0)

    lax.fori_loop(0, 2, batch, 0)
    accumulate(0, 480)
    lax.fori_loop(2, 5, batch, 0)
    accumulate(480, 720)
    lax.fori_loop(5, 8, batch, 0)

    def target(i):
        return {"region": colour * 2 + core, "tile": i}

    def p_copy(i, count):
        return pltpu.make_async_remote_copy(
            src_ref=psend.at[i, pl.ds(0, count)], dst_ref=precv.at[tile, pl.ds(0, count)],
            send_sem=ps_sem.at[i], recv_sem=pr_sem.at[tile], device_id=target(i))

    def v_copy(i):
        return pltpu.make_async_remote_copy(
            src_ref=vsend.at[i // 2], dst_ref=vrecv.at[tile],
            send_sem=vs_sem.at[i], recv_sem=vr_sem.at[tile], device_id=target(i))

    def d_copy(i):
        return pltpu.make_async_remote_copy(
            src_ref=dsend.at[i], dst_ref=drecv.at[tile],
            send_sem=ds_sem.at[i], recv_sem=dr_sem.at[tile], device_id=target(i))

    def is_self(i):
        return jnp.logical_and(own_worker, i == tile)

    for p in range(BR):
        vsend[p] = v_acc[p : p + 1, :]

    def turn(s):
        return jnp.where(s == 0, 1, jnp.where(s == 1, 3, jnp.where(s == 2, 2, 0)))

    def piece(s, carry):
        yy = (y + turn(s)) % 4
        prod = p_acc[yy] + product(yy, 1200, 720)
        for e in range(2):
            part = -prod[128 * e : 128 * e + 128, 128 * e : 128 * e + 640]
            d_acc[pl.ds(pl.multiple_of(yy * 256 + 128 * e, 128), 128), :] = part[:, :128]
            part = part.astype(BF16)
            for u in range(2):
                for j in range(4):
                    psend[yy * 4 + e * 2 + u, j] = part[ROWS * u : ROWS * u + ROWS, BS * (j + 1) : BS * (j + 2)]
        for u in (1, 3, 2, 0):
            i = yy * 4 + (x + u) % 4
            other = jnp.logical_not(is_self(i))

            @pl.when(jnp.logical_and(other, yy < 2))
            def _():
                p_copy(i, 4).start()

            @pl.when(jnp.logical_and(other, yy >= 2))
            def _():
                p_copy(i, 3).start()

            @pl.when(other)
            def _():
                v_copy(i).start()

            @pl.when(is_self(i))
            def _():
                precv[tile] = psend[i]
                vrecv[tile] = vsend[i // 2]
        return carry

    lax.fori_loop(0, 4, piece, 0)

    def diagonal(m, carry):
        found = [group_of(m // 2, m % 2 * 3 + q) for q in range(3)]
        g = jnp.concatenate([grecv[k, t].reshape(GROUP * HITS, BS) for k, t in found], axis=0)
        gt = jnp.transpose(g)
        wp = wp_buf[m]
        for p in range(BR):
            lhs[BS * p : BS * p + BS, :] = gt * wp[p : p + 1, :]
        d_acc[...] += jnp.dot(lhs[...], g, preferred_element_type=F32)
        return carry

    lax.fori_loop(0, CHUNKS, diagonal, 0)

    def send_diagonal(s, carry):
        i = (y + turn(s // 4)) % 4 * 4 + (x + turn(s % 4)) % 4
        dsend[i] = d_acc[pl.ds(pl.multiple_of(i * ROWS, ROWS), ROWS), :].astype(BF16)

        @pl.when(jnp.logical_not(is_self(i)))
        def _():
            d_copy(i).start()

        @pl.when(is_self(i))
        def _():
            drecv[tile] = dsend[i]
        return carry

    lax.fori_loop(0, 16, send_diagonal, 0)

    def p_arrival(i, count):
        return pltpu.make_async_remote_copy(
            src_ref=psend.at[0, pl.ds(0, count)], dst_ref=precv.at[i, pl.ds(0, count)],
            send_sem=ps_sem.at[0], recv_sem=pr_sem.at[i], device_id=sibling)

    def collect(i, carry):
        other = jnp.logical_not(is_self(i))

        @pl.when(jnp.logical_and(other, mine < 4))
        def _():
            p_arrival(i, 4).wait_recv()

        @pl.when(jnp.logical_and(other, mine >= 4))
        def _():
            p_arrival(i, 3).wait_recv()

        @pl.when(other)
        def _():
            pltpu.make_async_remote_copy(
                src_ref=vsend.at[0], dst_ref=vrecv.at[i], send_sem=vs_sem.at[0],
                recv_sem=vr_sem.at[i], device_id=sibling).wait_recv()
        return carry

    lax.fori_loop(0, 16, collect, 0)

    def x_copy(j, e):
        k = 2 * j - 2 + e
        return pltpu.make_async_remote_copy(
            src_ref=xsend.at[k], dst_ref=xrecv.at[2 * j - 2 + tile % 2],
            send_sem=xs_sem.at[k], recv_sem=xr_sem.at[2 * j - 2 + tile % 2], device_id=owner(mine + j, e))

    def x_arrival(j, e):
        k = 2 * j - 2 + e
        return pltpu.make_async_remote_copy(
            src_ref=xsend.at[k], dst_ref=xrecv.at[k],
            send_sem=xs_sem.at[k], recv_sem=xr_sem.at[k], device_id=sibling)

    def column(b):
        return pl.ds(pl.multiple_of(((b + 8) % 8) * BS, BS), BS)

    def reduce_block(j):
        total = precv[0, j - 1].astype(F32)
        for i in range(1, 16):
            total = total + precv[i, j - 1].astype(F32)
        out_ref[0, :, column(mine + j)] = total
        turned = jnp.transpose(total)
        for e in range(2):
            t = turned[ROWS * e : ROWS * e + ROWS]
            xsend[2 * j - 2 + e] = jnp.concatenate([t[:32], t[32:]], axis=1).astype(BF16)
            x_copy(j, e).start()

    def receive_block(j):
        for e in range(2):
            x_arrival(j, e).wait_recv()
        q0, q1 = xrecv[2 * j - 2].astype(F32), xrecv[2 * j - 1].astype(F32)
        out_ref[0, 0:32, column(mine - j)] = jnp.concatenate([q0[:, :ROWS], q1[:, :ROWS]], axis=1)
        out_ref[0, 32:64, column(mine - j)] = jnp.concatenate([q0[:, ROWS:], q1[:, ROWS:]], axis=1)

    @pl.when(mine < 4)
    def _():
        reduce_block(4)

    for j in range(3, 0, -1):
        reduce_block(j)

    row = vrecv[0]
    for i in range(1, 16):
        row = row + vrecv[i]
    vec_ref[...] = jnp.where(tile % 2 == 0, row[:, :ROWS], row[:, ROWS:])

    def collect_diagonal(i, carry):
        @pl.when(jnp.logical_not(is_self(i)))
        def _():
            pltpu.make_async_remote_copy(
                src_ref=dsend.at[0], dst_ref=drecv.at[i], send_sem=ds_sem.at[0],
                recv_sem=dr_sem.at[i], device_id=sibling).wait_recv()
        return carry

    lax.fori_loop(0, 16, collect_diagonal, 0)
    total = drecv[0].astype(F32)
    for i in range(1, 16):
        total = total + drecv[i].astype(F32)
    out_ref[0, :, column(mine)] = total

    for j in range(1, 4):
        receive_block(j)

    @pl.when(mine >= 4)
    def _():
        receive_block(4)

    for j in range(1, 4):
        for e in range(2):
            x_copy(j, e).wait_send()

    @pl.when(mine < 4)
    def _():
        for e in range(2):
            x_copy(4, e).wait_send()

    for u in range(2):
        for d in range(6):
            for t in range(3):
                g_copy(d, u, t).wait_send()
            a_copy(d, u).wait_send()
    for h in range(2):
        for t in range(3):
            g_sib(h, t).wait_send()
        a_sib(h).wait_send()

    def finish(i, carry):
        other = jnp.logical_not(is_self(i))

        @pl.when(jnp.logical_and(other, i < 8))
        def _():
            p_copy(i, 4).wait_send()

        @pl.when(jnp.logical_and(other, i >= 8))
        def _():
            p_copy(i, 3).wait_send()

        @pl.when(other)
        def _():
            v_copy(i).wait_send()
            d_copy(i).wait_send()
        return carry

    lax.fori_loop(0, 16, finish, 0)


def local(
    global_deriv,
    local_deriv,
    hit_weight,
    hit_resid,
    block_ids,
    hit_count,
    track_region,
    block_place,
):
    vmem = pl.BlockSpec(memory_space=pltpu.VMEM)
    dma = pltpu.SemaphoreType.DMA
    return pl.pallas_call(
        kernel,
        name="assemble",
        out_shape=(
            jax.ShapeDtypeStruct((1, ROWS, WIDTH), F32),
            jax.ShapeDtypeStruct((1, ROWS), F32),
        ),
        in_specs=[pl.BlockSpec(memory_space=pltpu.SMEM)] + [vmem] * 7,
        out_specs=(vmem, vmem),
        scratch_shapes=[
            pltpu.SMEM((1, N_REGION * CAP), jnp.int32),
            pltpu.VMEM((BR, N_REGION * CAP), jnp.int32),
            pltpu.VMEM((14, 3, GROUP, HITS, BS), BF16),
            pltpu.VMEM((CHUNKS, 3, GROUP, HITS, BS), BF16),
            pltpu.VMEM((14, 3, GROUP, 256), BF16),
            pltpu.VMEM((CHUNKS, 3, GROUP, 256), BF16),
            pltpu.VMEM((TRK, 256), BF16),
            pltpu.VMEM((WIDTH, HALF * HITS), BF16),
            pltpu.VMEM((CHUNKS, BR, HALF * HITS), BF16),
            pltpu.VMEM((CHUNKS * 120, WIDTH + WIDTH // 2), BF16),
            pltpu.VMEM((4, 256, 768), F32),
            pltpu.VMEM((WIDTH, BS), F32),
            pltpu.VMEM((BR, BS), F32),
            pltpu.VMEM((BR, 1, BS), F32),
            pltpu.VMEM((16, 4, ROWS, BS), BF16),
            pltpu.VMEM((16, 4, ROWS, BS), BF16),
            pltpu.VMEM((16, 1, BS), F32),
            pltpu.VMEM((16, ROWS, BS), BF16),
            pltpu.VMEM((16, ROWS, BS), BF16),
            pltpu.VMEM((8, 32, BS), BF16),
            pltpu.VMEM((8, 32, BS), BF16),
            dma((14, 3)), dma((16, 3)), dma((14,)), dma((16,)),
            dma((16,)), dma((16,)), dma((16,)), dma((16,)), dma((16,)), dma((16,)), dma((8,)), dma((8,)), dma,
        ],
        compiler_params=pltpu.CompilerParams(
            collective_id=0, has_side_effects=True, vmem_limit_bytes=56 << 20),
    )(
        block_place, global_deriv, local_deriv.transpose(1, 2, 0), hit_weight.T, hit_resid.T,
        block_ids.T, hit_count.reshape(1, TRK), track_region.reshape(1, TRK))


def solution(mesh):
    return jax.shard_map(
        local,
        mesh=mesh,
        in_specs=(
            P(("region", "tile"), None, None),
            P(("region", "tile"), None, None),
            P(("region", "tile"), None),
            P(("region", "tile"), None),
            P(("region", "tile"), None),
            P(("region", "tile")),
            P(("region", "tile"), None),
            P(),
        ),
        out_specs=(P("region", "tile", None), P("region", "tile")),
        check_vma=False,
    )
```

```python
import functools

import jax
import jax.numpy as jnp
from jax import lax
from jax.experimental import pallas as pl
from jax.experimental.pallas import tpu as pltpu
from jax.sharding import PartitionSpec as P

BS = 128
BR = 8
HITS = 32
TRK = 192
CAP = 48
N_REGION = 8
HALF = CAP // 2
GROUP = 8
CHUNKS = 16
ROWS = 64
WIDTH = BR * BS
F32 = jnp.float32
BF16 = jnp.bfloat16
DIRS = (
    (1, 0, 0, 1, 0),
    (0, 0, 1, 1, 1),
    (-1, 0, 0, 3, 0),
    (0, 0, -1, 3, 1),
    (0, 1, 0, 2, 0),
    (0, -1, 0, 2, 1),
)


def fit(slopes, w, r, place):
    wl = [s * w for s in slopes]
    gamma = [[None] * 5 for _ in range(5)]
    for a in range(5):
        for b in range(a + 1):
            gamma[a][b] = jnp.sum(wl[a] * slopes[b], axis=0, keepdims=True) + (1.0 if a == b else 0.0)
    beta = [jnp.sum(wl[a] * r, axis=0, keepdims=True) for a in range(5)]
    factor = [[None] * 5 for _ in range(5)]
    inverse = [None] * 5
    for j in range(5):
        center = gamma[j][j]
        for k in range(j):
            center = center - factor[j][k] * factor[j][k]
        factor[j][j] = jnp.sqrt(center)
        inverse[j] = 1.0 / factor[j][j]
        for i in range(j + 1, 5):
            off = gamma[i][j]
            for k in range(j):
                off = off - factor[i][k] * factor[j][k]
            factor[i][j] = off * inverse[j]
    solved, target = [], []
    for j in range(5):
        cur, tgt = wl[j], beta[j]
        for k in range(j):
            cur = cur - factor[j][k] * solved[k]
            tgt = tgt - factor[j][k] * target[k]
        solved.append(cur * inverse[j])
        target.append(tgt * inverse[j])
    hit = w * r
    for k in range(5):
        hit = hit - solved[k] * target[k]
    full = jnp.concatenate(solved + [hit, w, place], axis=0)
    return jnp.transpose(full).astype(BF16)


def kernel(
    place_ref, g_ref, slope_ref, weight_ref, resid_ref, block_ref, count_ref, region_ref,
    out_ref, vec_ref, idx_ref, idx_vec,
    gsend, grecv, asend, arecv, fitted, lhs, wp_buf, s_buf, p_acc, d_acc, v_acc, vsend,
    psend, precv, vrecv, dsend, drecv, xsend, xrecv,
    gs_sem, gr_sem, as_sem, ar_sem, ps_sem, pr_sem, vs_sem, vr_sem, ds_sem, dr_sem, xs_sem, xr_sem, idx_sem, plane_sem, all_sem,
):
    region = lax.axis_index("region")
    tile = lax.axis_index("tile")
    z, core = region // 2, region % 2
    y, x = tile // 4, tile % 4
    colour = (x + 2 * y + z) % 4

    def device(nx, ny, nz, ncore):
        return {"region": nz * 2 + ncore, "tile": ny * 4 + nx}

    def neighbour(d, ncore):
        dx, dy, dz = DIRS[d][:3]
        return device((x + dx + 4) % 4, (y + dy + 4) % 4, (z + dz + 4) % 4, ncore)

    sibling = device(x, y, z, 1 - core)

    barrier = pltpu.get_barrier_semaphore()
    for d in range(6):
        for c in range(2):
            pl.semaphore_signal(barrier, inc=1, device_id=neighbour(d, c))
    pl.semaphore_signal(barrier, inc=1, device_id=sibling)

    def along(axis, k):
        steps = [k if axis == n else 0 for n in range(3)]
        return device((x + steps[0]) % 4, (y + steps[1]) % 4, (z + steps[2]) % 4, core)

    for axis in range(3):
        pl.semaphore_signal(barrier, inc=1, device_id=along(axis, 2))

    own_worker = (x + 2 * y) % 4 == 0
    mine = tile // 2

    def owner(a, e):
        return {"region": region, "tile": ((a + 8) % 8) * 2 + e}

    def tell(sem, axis):
        for k in range(1, 4):
            pl.semaphore_signal(sem, inc=1, device_id=along(axis, k))

    reg = region_ref[...]
    tracks8 = lax.broadcasted_iota(jnp.int32, (BR, TRK), 0)
    named = jnp.where(reg == tracks8, 1.0, 0.0)
    earlier = (
        lax.broadcasted_iota(jnp.int32, (TRK, TRK), 0) < lax.broadcasted_iota(jnp.int32, (TRK, TRK), 1))
    ahead = jnp.dot(named.astype(BF16), jnp.where(earlier, 1.0, 0.0).astype(BF16), preferred_element_type=F32)
    slot = reg.astype(F32) * CAP + jnp.sum(named * ahead, axis=0, keepdims=True)
    slot_col = jnp.transpose(jnp.broadcast_to(slot, (BR, TRK)))[:, 0:1]
    slot_lane = lax.broadcasted_iota(jnp.int32, (TRK, N_REGION * CAP), 1).astype(F32)
    onehot = jnp.where(slot_col == slot_lane, 1.0, 0.0).astype(BF16)
    number = lax.broadcasted_iota(jnp.int32, (BR, TRK), 1).astype(F32).astype(BF16)
    idx_vec[...] = jnp.dot(number, onehot, preferred_element_type=F32).astype(jnp.int32)
    idx_copy = pltpu.make_async_copy(idx_vec.at[pl.ds(0, 1)], idx_ref, idx_sem)
    idx_copy.start()
    idx_copy.wait()

    def gather(q, t, ref, k):
        for i in range(GROUP):
            ref[k, t, i] = g_ref[jnp.clip(idx_ref[0, q * HALF + t * GROUP + i], 0, TRK - 1)]

    def chunk_of(d, c):
        step, half = DIRS[d][3:]
        return (((colour + step) % 4) * 2 + c) * 2 + half

    def g_copy(d, u, t):
        k = u * 6 + d
        return pltpu.make_async_remote_copy(
            src_ref=gsend.at[k, t], dst_ref=grecv.at[k, t],
            send_sem=gs_sem.at[k, t], recv_sem=gr_sem.at[k, t],
            device_id=neighbour(d, core ^ u))

    def a_copy(d, u):
        k = u * 6 + d
        return pltpu.make_async_remote_copy(
            src_ref=asend.at[k], dst_ref=arecv.at[k],
            send_sem=as_sem.at[k], recv_sem=ar_sem.at[k],
            device_id=neighbour(d, core ^ u))

    def g_sib(h, t):
        return pltpu.make_async_remote_copy(
            src_ref=gsend.at[12 + h, t], dst_ref=grecv.at[12 + 2 * core + h, t],
            send_sem=gs_sem.at[12 + h, t], recv_sem=gr_sem.at[12 + 2 * core + h, t],
            device_id=sibling)

    def a_sib(h):
        return pltpu.make_async_remote_copy(
            src_ref=asend.at[12 + h], dst_ref=arecv.at[12 + 2 * core + h],
            send_sem=as_sem.at[12 + h], recv_sem=ar_sem.at[12 + 2 * core + h],
            device_id=sibling)

    def send_tracks(u):
        for t in range(3):
            for d in range(6):
                gather(chunk_of(d, core ^ u), t, gsend, u * 6 + d)
                if u == 0 and t == 0 and d == 0:
                    pl.semaphore_wait(barrier, 16)
                g_copy(d, u, t).start()

    send_tracks(0)
    tell(plane_sem, 1)

    live = lax.broadcasted_iota(jnp.int32, (HITS, TRK), 0) < count_ref[...]
    weight = jnp.where(live, weight_ref[...].astype(F32), 0.0)
    ids = block_ref[...]
    place = jnp.zeros((HITS, TRK), F32)
    for b in range(BR):
        place = jnp.where(ids == b, place_ref[b].astype(F32), place)
    fitted[...] = fit(
        [slope_ref[c].astype(F32) for c in range(5)], weight, resid_ref[...].astype(F32), place)

    def pick(q, ref, k):
        rows = (q * HALF + lax.broadcasted_iota(jnp.int32, (HALF, TRK), 0)).astype(F32)
        chosen = jnp.where(slot == rows, 1.0, 0.0).astype(BF16)
        picked = jnp.dot(chosen, fitted[...], preferred_element_type=F32)
        for t in range(3):
            ref[k, t] = picked[GROUP * t : GROUP * t + GROUP].astype(BF16)

    for u in range(2):
        for d in range(6):
            pick(chunk_of(d, core ^ u), asend, u * 6 + d)
            a_copy(d, u).start()
    for h in range(2):
        pick((colour * 2 + 1 - core) * 2 + h, asend, 12 + h)
        a_sib(h).start()
    send_tracks(1)
    pl.semaphore_wait(plane_sem, 3)
    tell(all_sem, 0)
    for h in range(2):
        for t in range(3):
            gather((colour * 2 + 1 - core) * 2 + h, t, gsend, 12 + h)
            g_sib(h, t).start()
    for h in range(2):
        pick((colour * 2 + core) * 2 + h, arecv, 12 + 2 * core + h)
        for t in range(3):
            gather((colour * 2 + core) * 2 + h, t, grecv, 12 + 2 * core + h)

    v_acc[...] = jnp.zeros_like(v_acc)

    lane = lax.broadcasted_iota(jnp.int32, (GROUP, 128), 1)
    track = lax.broadcasted_iota(jnp.int32, (GROUP, 128), 0)
    residue = track % 4
    blocks = [(lane // HITS + 4 * v) == track for v in range(2)]
    subf = lax.broadcasted_iota(jnp.int32, (GROUP, 256), 0).astype(F32)

    def group_of(m, q):
        far = m - 2
        source = jnp.where(m == 0, core, 1 - core)
        k = jnp.where(m < 2, 12 + 2 * source + q // 3, far // 3 * 6 + q)
        return k, jnp.where(m < 2, q % 3, far % 3)

    def batch(m, carry):
        found = [group_of(m, q) for q in range(6)]

        @pl.when(m >= 1)
        def _():
            for k, t in found:
                pltpu.make_async_remote_copy(
                    src_ref=gsend.at[0, 0], dst_ref=grecv.at[k, t], send_sem=gs_sem.at[0, 0],
                    recv_sem=gr_sem.at[k, t], device_id=sibling).wait_recv()

        def aux_arrival(k):
            pltpu.make_async_remote_copy(
                src_ref=asend.at[0], dst_ref=arecv.at[k], send_sem=as_sem.at[0],
                recv_sem=ar_sem.at[k], device_id=sibling).wait_recv()

        @pl.when(m == 1)
        def _():
            for h in range(2):
                aux_arrival(12 + 2 * (1 - core) + h)

        @pl.when(jnp.logical_and(m >= 2, (m - 2) % 3 == 0))
        def _():
            for d in range(6):
                aux_arrival((m - 2) // 3 * 6 + d)

        parts, wps = [], []
        vec = None
        for k, t in found:
            aj = arecv[k, t].astype(F32)
            gj = grecv[k, t].reshape(GROUP * HITS, BS)
            turned = []
            for v in range(2):
                half = aj[:, 128 * v : 128 * v + 128]
                turned.append([half] + [pltpu.roll(half, HITS * k, 1) for k in range(1, 4)])

            def spread_lanes(q):
                options = turned[q // 4]
                own_turn = options[(3 - q) % 4]
                for k in range(3):
                    own_turn = jnp.where(residue == k, options[(k - q) % 4], own_turn)
                return jnp.concatenate([jnp.where(b, own_turn, 0.0) for b in blocks], axis=1)

            place = spread_lanes(7)
            base = [spread_lanes(q) for q in range(5)]
            rows = []
            for p in range(BR):
                here = place == float(p)
                rows.extend(jnp.where(here, b, 0.0) for b in base)
            left = jnp.concatenate(rows, axis=0).astype(BF16)
            parts.append(jnp.dot(left, gj, preferred_element_type=F32))
            prow = jnp.sum(place, axis=0, keepdims=True)
            hrow = jnp.sum(spread_lanes(5), axis=0, keepdims=True)
            wrow = jnp.sum(spread_lanes(6), axis=0, keepdims=True)
            onp = subf == prow
            vj = jnp.dot(jnp.where(onp, hrow, 0.0).astype(BF16), gj, preferred_element_type=F32)
            vec = vj if vec is None else vec + vj
            wps.append(jnp.where(onp, wrow, 0.0).astype(BF16))
        v_acc[...] += vec
        for h in range(2):
            wp_buf[2 * m + h] = jnp.concatenate(wps[3 * h : 3 * h + 3], axis=1)
        rows = pl.ds(pl.multiple_of(m * 240, 16), 240)
        for p in range(BR):
            piece = jnp.concatenate([q[40 * p : 40 * p + 40] for q in parts], axis=0).astype(BF16)
            s_buf[rows, BS * p : BS * p + BS] = piece
            if p < 4:
                s_buf[rows, WIDTH + BS * p : WIDTH + BS * p + BS] = piece
        return carry

    def product(yy, first, count):
        start = pl.multiple_of(yy * 256, 256)
        return lax.dot_general(
            s_buf[first : first + count, pl.ds(start, 256)], s_buf[first : first + count, pl.ds(start, 768)],
            (((0,), (0,)), ((), ())), preferred_element_type=F32)

    def accumulate(first, count):
        def body(yy, carry):
            p = product(yy, first, count)
            p_acc[yy] = p if first == 0 else p_acc[yy] + p
            return carry
        lax.fori_loop(0, 4, body, 0)

    lax.fori_loop(0, 2, batch, 0)
    accumulate(0, 480)
    lax.fori_loop(2, 5, batch, 0)
    accumulate(480, 720)
    lax.fori_loop(5, 8, batch, 0)
    pl.semaphore_wait(all_sem, 3)

    def target(i):
        return {"region": colour * 2 + core, "tile": i}

    def p_copy(i, count):
        return pltpu.make_async_remote_copy(
            src_ref=psend.at[i, pl.ds(0, count)], dst_ref=precv.at[tile, pl.ds(0, count)],
            send_sem=ps_sem.at[i], recv_sem=pr_sem.at[tile], device_id=target(i))

    def v_copy(i):
        return pltpu.make_async_remote_copy(
            src_ref=vsend.at[i // 2], dst_ref=vrecv.at[tile],
            send_sem=vs_sem.at[i], recv_sem=vr_sem.at[tile], device_id=target(i))

    def d_copy(i):
        return pltpu.make_async_remote_copy(
            src_ref=dsend.at[i], dst_ref=drecv.at[tile],
            send_sem=ds_sem.at[i], recv_sem=dr_sem.at[tile], device_id=target(i))

    def is_self(i):
        return jnp.logical_and(own_worker, i == tile)

    for p in range(BR):
        vsend[p] = v_acc[p : p + 1, :]

    def turn(s):
        return jnp.where(s == 0, 1, jnp.where(s == 1, 3, jnp.where(s == 2, 2, 0)))

    def piece(s, carry):
        yy = (y + turn(s)) % 4
        prod = p_acc[yy] + product(yy, 1200, 720)
        for e in range(2):
            part = -prod[128 * e : 128 * e + 128, 128 * e : 128 * e + 640]
            d_acc[pl.ds(pl.multiple_of(yy * 256 + 128 * e, 128), 128), :] = part[:, :128]
            part = part.astype(BF16)
            for u in range(2):
                for j in range(4):
                    psend[yy * 4 + e * 2 + u, j] = part[ROWS * u : ROWS * u + ROWS, BS * (j + 1) : BS * (j + 2)]
        for u in (1, 3, 2, 0):
            i = yy * 4 + (x + u) % 4
            other = jnp.logical_not(is_self(i))

            @pl.when(jnp.logical_and(other, yy < 2))
            def _():
                p_copy(i, 4).start()

            @pl.when(jnp.logical_and(other, yy >= 2))
            def _():
                p_copy(i, 3).start()

            @pl.when(other)
            def _():
                v_copy(i).start()

            @pl.when(is_self(i))
            def _():
                precv[tile] = psend[i]
                vrecv[tile] = vsend[i // 2]
        return carry

    lax.fori_loop(0, 4, piece, 0)

    def diagonal(m, carry):
        found = [group_of(m // 2, m % 2 * 3 + q) for q in range(3)]
        g = jnp.concatenate([grecv[k, t].reshape(GROUP * HITS, BS) for k, t in found], axis=0)
        gt = jnp.transpose(g)
        wp = wp_buf[m]
        for p in range(BR):
            lhs[BS * p : BS * p + BS, :] = gt * wp[p : p + 1, :]
        d_acc[...] += jnp.dot(lhs[...], g, preferred_element_type=F32)
        return carry

    lax.fori_loop(0, CHUNKS, diagonal, 0)

    def send_diagonal(s, carry):
        i = (y + turn(s // 4)) % 4 * 4 + (x + turn(s % 4)) % 4
        dsend[i] = d_acc[pl.ds(pl.multiple_of(i * ROWS, ROWS), ROWS), :].astype(BF16)

        @pl.when(jnp.logical_not(is_self(i)))
        def _():
            d_copy(i).start()

        @pl.when(is_self(i))
        def _():
            drecv[tile] = dsend[i]
        return carry

    lax.fori_loop(0, 16, send_diagonal, 0)

    def p_arrival(i, count):
        return pltpu.make_async_remote_copy(
            src_ref=psend.at[0, pl.ds(0, count)], dst_ref=precv.at[i, pl.ds(0, count)],
            send_sem=ps_sem.at[0], recv_sem=pr_sem.at[i], device_id=sibling)

    def collect(i, carry):
        other = jnp.logical_not(is_self(i))

        @pl.when(jnp.logical_and(other, mine < 4))
        def _():
            p_arrival(i, 4).wait_recv()

        @pl.when(jnp.logical_and(other, mine >= 4))
        def _():
            p_arrival(i, 3).wait_recv()

        @pl.when(other)
        def _():
            pltpu.make_async_remote_copy(
                src_ref=vsend.at[0], dst_ref=vrecv.at[i], send_sem=vs_sem.at[0],
                recv_sem=vr_sem.at[i], device_id=sibling).wait_recv()
        return carry

    lax.fori_loop(0, 16, collect, 0)

    def x_copy(j, e):
        k = 2 * j - 2 + e
        return pltpu.make_async_remote_copy(
            src_ref=xsend.at[k], dst_ref=xrecv.at[2 * j - 2 + tile % 2],
            send_sem=xs_sem.at[k], recv_sem=xr_sem.at[2 * j - 2 + tile % 2], device_id=owner(mine + j, e))

    def x_arrival(j, e):
        k = 2 * j - 2 + e
        return pltpu.make_async_remote_copy(
            src_ref=xsend.at[k], dst_ref=xrecv.at[k],
            send_sem=xs_sem.at[k], recv_sem=xr_sem.at[k], device_id=sibling)

    def column(b):
        return pl.ds(pl.multiple_of(((b + 8) % 8) * BS, BS), BS)

    def reduce_block(j):
        total = precv[0, j - 1].astype(F32)
        for i in range(1, 16):
            total = total + precv[i, j - 1].astype(F32)
        out_ref[0, :, column(mine + j)] = total
        turned = jnp.transpose(total)
        for e in range(2):
            t = turned[ROWS * e : ROWS * e + ROWS]
            xsend[2 * j - 2 + e] = jnp.concatenate([t[:32], t[32:]], axis=1).astype(BF16)
            x_copy(j, e).start()

    def receive_block(j):
        for e in range(2):
            x_arrival(j, e).wait_recv()
        q0, q1 = xrecv[2 * j - 2].astype(F32), xrecv[2 * j - 1].astype(F32)
        out_ref[0, 0:32, column(mine - j)] = jnp.concatenate([q0[:, :ROWS], q1[:, :ROWS]], axis=1)
        out_ref[0, 32:64, column(mine - j)] = jnp.concatenate([q0[:, ROWS:], q1[:, ROWS:]], axis=1)

    @pl.when(mine < 4)
    def _():
        reduce_block(4)

    for j in range(3, 0, -1):
        reduce_block(j)

    row = vrecv[0]
    for i in range(1, 16):
        row = row + vrecv[i]
    vec_ref[...] = jnp.where(tile % 2 == 0, row[:, :ROWS], row[:, ROWS:])

    def collect_diagonal(i, carry):
        @pl.when(jnp.logical_not(is_self(i)))
        def _():
            pltpu.make_async_remote_copy(
                src_ref=dsend.at[0], dst_ref=drecv.at[i], send_sem=ds_sem.at[0],
                recv_sem=dr_sem.at[i], device_id=sibling).wait_recv()
        return carry

    lax.fori_loop(0, 16, collect_diagonal, 0)
    total = drecv[0].astype(F32)
    for i in range(1, 16):
        total = total + drecv[i].astype(F32)
    out_ref[0, :, column(mine)] = total

    for j in range(1, 4):
        receive_block(j)

    @pl.when(mine >= 4)
    def _():
        receive_block(4)

    for j in range(1, 4):
        for e in range(2):
            x_copy(j, e).wait_send()

    @pl.when(mine < 4)
    def _():
        for e in range(2):
            x_copy(4, e).wait_send()

    for u in range(2):
        for d in range(6):
            for t in range(3):
                g_copy(d, u, t).wait_send()
            a_copy(d, u).wait_send()
    for h in range(2):
        for t in range(3):
            g_sib(h, t).wait_send()
        a_sib(h).wait_send()

    def finish(i, carry):
        other = jnp.logical_not(is_self(i))

        @pl.when(jnp.logical_and(other, i < 8))
        def _():
            p_copy(i, 4).wait_send()

        @pl.when(jnp.logical_and(other, i >= 8))
        def _():
            p_copy(i, 3).wait_send()

        @pl.when(other)
        def _():
            v_copy(i).wait_send()
            d_copy(i).wait_send()
        return carry

    lax.fori_loop(0, 16, finish, 0)


def hand_over(matrix_ref, vector_ref, out_ref, vec_ref):
    out_ref[...] = matrix_ref[...]
    vec_ref[...] = vector_ref[...]


def local(
    global_deriv,
    local_deriv,
    hit_weight,
    hit_resid,
    block_ids,
    hit_count,
    track_region,
    block_place,
):
    vmem = pl.BlockSpec(memory_space=pltpu.VMEM)
    dma = pltpu.SemaphoreType.DMA
    matrix, vector = pl.pallas_call(
        kernel,
        name="assemble",
        out_shape=(
            jax.ShapeDtypeStruct((1, ROWS, WIDTH), F32),
            jax.ShapeDtypeStruct((1, ROWS), F32),
        ),
        in_specs=[pl.BlockSpec(memory_space=pltpu.SMEM)] + [vmem] * 7,
        out_specs=(vmem, vmem),
        scratch_shapes=[
            pltpu.SMEM((1, N_REGION * CAP), jnp.int32),
            pltpu.VMEM((BR, N_REGION * CAP), jnp.int32),
            pltpu.VMEM((14, 3, GROUP, HITS, BS), BF16),
            pltpu.VMEM((CHUNKS, 3, GROUP, HITS, BS), BF16),
            pltpu.VMEM((14, 3, GROUP, 256), BF16),
            pltpu.VMEM((CHUNKS, 3, GROUP, 256), BF16),
            pltpu.VMEM((TRK, 256), BF16),
            pltpu.VMEM((WIDTH, HALF * HITS), BF16),
            pltpu.VMEM((CHUNKS, BR, HALF * HITS), BF16),
            pltpu.VMEM((CHUNKS * 120, WIDTH + WIDTH // 2), BF16),
            pltpu.VMEM((4, 256, 768), F32),
            pltpu.VMEM((WIDTH, BS), F32),
            pltpu.VMEM((BR, BS), F32),
            pltpu.VMEM((BR, 1, BS), F32),
            pltpu.VMEM((16, 4, ROWS, BS), BF16),
            pltpu.VMEM((16, 4, ROWS, BS), BF16),
            pltpu.VMEM((16, 1, BS), F32),
            pltpu.VMEM((16, ROWS, BS), BF16),
            pltpu.VMEM((16, ROWS, BS), BF16),
            pltpu.VMEM((8, 32, BS), BF16),
            pltpu.VMEM((8, 32, BS), BF16),
            dma((14, 3)), dma((16, 3)), dma((14,)), dma((16,)),
            dma((16,)), dma((16,)), dma((16,)), dma((16,)), dma((16,)), dma((16,)), dma((8,)), dma((8,)), dma,
            pltpu.SemaphoreType.REGULAR, pltpu.SemaphoreType.REGULAR,
        ],
        compiler_params=pltpu.CompilerParams(
            collective_id=0, has_side_effects=True, vmem_limit_bytes=56 << 20),
    )(
        block_place, global_deriv, local_deriv.transpose(1, 2, 0), hit_weight.T, hit_resid.T,
        block_ids.T, hit_count.reshape(1, TRK), track_region.reshape(1, TRK))
    return pl.pallas_call(
        hand_over,
        name="hand_over",
        out_shape=(
            jax.ShapeDtypeStruct((1, ROWS, WIDTH), F32),
            jax.ShapeDtypeStruct((1, ROWS), F32),
        ),
        in_specs=[vmem, vmem],
        out_specs=(vmem, vmem),
    )(matrix, vector)


def solution(mesh):
    return jax.shard_map(
        local,
        mesh=mesh,
        in_specs=(
            P(("region", "tile"), None, None),
            P(("region", "tile"), None, None),
            P(("region", "tile"), None),
            P(("region", "tile"), None),
            P(("region", "tile"), None),
            P(("region", "tile")),
            P(("region", "tile"), None),
            P(),
        ),
        out_specs=(P("region", "tile", None), P("region", "tile")),
        check_vma=False,
    )
```

```python
import functools

import jax
import jax.numpy as jnp
from jax import lax
from jax.experimental import pallas as pl
from jax.experimental.pallas import tpu as pltpu
from jax.sharding import PartitionSpec as P

BS = 128
BR = 8
HITS = 32
TRK = 192
CAP = 48
N_REGION = 8
HALF = CAP // 2
GROUP = 8
CHUNKS = 16
ROWS = 64
WIDTH = BR * BS
F32 = jnp.float32
BF16 = jnp.bfloat16
DIRS = (
    (1, 0, 0, 1, 0),
    (0, 0, 1, 1, 1),
    (-1, 0, 0, 3, 0),
    (0, 0, -1, 3, 1),
    (0, 1, 0, 2, 0),
    (0, -1, 0, 2, 1),
)


def fit(slopes, w, r, place):
    wl = [s * w for s in slopes]
    gamma = [[None] * 5 for _ in range(5)]
    for a in range(5):
        for b in range(a + 1):
            gamma[a][b] = jnp.sum(wl[a] * slopes[b], axis=0, keepdims=True) + (1.0 if a == b else 0.0)
    beta = [jnp.sum(wl[a] * r, axis=0, keepdims=True) for a in range(5)]
    factor = [[None] * 5 for _ in range(5)]
    inverse = [None] * 5
    for j in range(5):
        center = gamma[j][j]
        for k in range(j):
            center = center - factor[j][k] * factor[j][k]
        factor[j][j] = jnp.sqrt(center)
        inverse[j] = 1.0 / factor[j][j]
        for i in range(j + 1, 5):
            off = gamma[i][j]
            for k in range(j):
                off = off - factor[i][k] * factor[j][k]
            factor[i][j] = off * inverse[j]
    solved, target = [], []
    for j in range(5):
        cur, tgt = wl[j], beta[j]
        for k in range(j):
            cur = cur - factor[j][k] * solved[k]
            tgt = tgt - factor[j][k] * target[k]
        solved.append(cur * inverse[j])
        target.append(tgt * inverse[j])
    hit = w * r
    for k in range(5):
        hit = hit - solved[k] * target[k]
    full = jnp.concatenate(solved + [hit, w, place], axis=0)
    return jnp.transpose(full).astype(BF16)


def kernel(
    place_ref, g_ref, slope_ref, weight_ref, resid_ref, block_ref, count_ref, region_ref,
    out_ref, vec_ref, idx_ref, idx_vec,
    gsend, grecv, asend, arecv, fitted, lhs, wp_buf, s_buf, p_acc, d_acc, v_acc, vsend,
    psend, precv, vrecv, dsend, drecv, xsend, xrecv,
    gs_sem, gr_sem, as_sem, ar_sem, ps_sem, pr_sem, vs_sem, vr_sem, ds_sem, dr_sem, xs_sem, xr_sem, idx_sem, pair_sem, plane_sem, all_sem,
):
    region = lax.axis_index("region")
    tile = lax.axis_index("tile")
    z, core = region // 2, region % 2
    y, x = tile // 4, tile % 4
    colour = (x + 2 * y + z) % 4

    def device(nx, ny, nz, ncore):
        return {"region": nz * 2 + ncore, "tile": ny * 4 + nx}

    def neighbour(d, ncore):
        dx, dy, dz = DIRS[d][:3]
        return device((x + dx + 4) % 4, (y + dy + 4) % 4, (z + dz + 4) % 4, ncore)

    sibling = device(x, y, z, 1 - core)

    barrier = pltpu.get_barrier_semaphore()
    for d in range(6):
        pl.semaphore_signal(barrier, inc=1, device_id=neighbour(d, core))
    pl.semaphore_signal(barrier, inc=1, device_id=sibling)

    def along(axis, k):
        steps = [k if axis == n else 0 for n in range(3)]
        return device((x + steps[0]) % 4, (y + steps[1]) % 4, (z + steps[2]) % 4, core)

    for axis in range(3):
        pl.semaphore_signal(barrier, inc=1, device_id=along(axis, 2))

    own_worker = (x + 2 * y) % 4 == 0
    mine = tile // 2

    def owner(a, e):
        return {"region": region, "tile": ((a + 8) % 8) * 2 + e}

    def tell(sem, axis):
        for k in range(1, 4):
            pl.semaphore_signal(sem, inc=1, device_id=along(axis, k))

    reg = region_ref[...]
    tracks8 = lax.broadcasted_iota(jnp.int32, (BR, TRK), 0)
    named = jnp.where(reg == tracks8, 1.0, 0.0)
    earlier = (
        lax.broadcasted_iota(jnp.int32, (TRK, TRK), 0) < lax.broadcasted_iota(jnp.int32, (TRK, TRK), 1))
    ahead = jnp.dot(named.astype(BF16), jnp.where(earlier, 1.0, 0.0).astype(BF16), preferred_element_type=F32)
    slot = reg.astype(F32) * CAP + jnp.sum(named * ahead, axis=0, keepdims=True)
    slot_col = jnp.transpose(jnp.broadcast_to(slot, (BR, TRK)))[:, 0:1]
    slot_lane = lax.broadcasted_iota(jnp.int32, (TRK, N_REGION * CAP), 1).astype(F32)
    onehot = jnp.where(slot_col == slot_lane, 1.0, 0.0).astype(BF16)
    number = lax.broadcasted_iota(jnp.int32, (BR, TRK), 1).astype(F32).astype(BF16)
    idx_vec[...] = jnp.dot(number, onehot, preferred_element_type=F32).astype(jnp.int32)
    idx_copy = pltpu.make_async_copy(idx_vec.at[pl.ds(0, 1)], idx_ref, idx_sem)
    idx_copy.start()
    idx_copy.wait()

    def gather(q, t, ref, k):
        for i in range(GROUP):
            ref[k, t, i] = g_ref[jnp.clip(idx_ref[0, q * HALF + t * GROUP + i], 0, TRK - 1)]

    def chunk_of(d, c):
        step, half = DIRS[d][3:]
        return (((colour + step) % 4) * 2 + c) * 2 + half

    def g_copy(d, u, t):
        k = u * 6 + d
        return pltpu.make_async_remote_copy(
            src_ref=gsend.at[k, t], dst_ref=grecv.at[k, t],
            send_sem=gs_sem.at[k, t], recv_sem=gr_sem.at[k, t],
            device_id=neighbour(d, core ^ u))

    def a_copy(d, u):
        k = u * 6 + d
        return pltpu.make_async_remote_copy(
            src_ref=asend.at[k], dst_ref=arecv.at[k],
            send_sem=as_sem.at[k], recv_sem=ar_sem.at[k],
            device_id=neighbour(d, core ^ u))

    def g_sib(h, t):
        return pltpu.make_async_remote_copy(
            src_ref=gsend.at[12 + h, t], dst_ref=grecv.at[12 + 2 * core + h, t],
            send_sem=gs_sem.at[12 + h, t], recv_sem=gr_sem.at[12 + 2 * core + h, t],
            device_id=sibling)

    def a_sib(h):
        return pltpu.make_async_remote_copy(
            src_ref=asend.at[12 + h], dst_ref=arecv.at[12 + 2 * core + h],
            send_sem=as_sem.at[12 + h], recv_sem=ar_sem.at[12 + 2 * core + h],
            device_id=sibling)

    def send_tracks(u):
        for t in range(3):
            for d in range(6):
                gather(chunk_of(d, core ^ u), t, gsend, u * 6 + d)
                if u == 0 and t == 0 and d == 0:
                    pl.semaphore_wait(barrier, 10)
                g_copy(d, u, t).start()

    send_tracks(0)
    pl.semaphore_signal(pair_sem, inc=1, device_id=sibling)
    tell(plane_sem, 1)

    live = lax.broadcasted_iota(jnp.int32, (HITS, TRK), 0) < count_ref[...]
    weight = jnp.where(live, weight_ref[...].astype(F32), 0.0)
    ids = block_ref[...]
    place = jnp.zeros((HITS, TRK), F32)
    for b in range(BR):
        place = jnp.where(ids == b, place_ref[b].astype(F32), place)
    fitted[...] = fit(
        [slope_ref[c].astype(F32) for c in range(5)], weight, resid_ref[...].astype(F32), place)

    def pick(q, ref, k):
        rows = (q * HALF + lax.broadcasted_iota(jnp.int32, (HALF, TRK), 0)).astype(F32)
        chosen = jnp.where(slot == rows, 1.0, 0.0).astype(BF16)
        picked = jnp.dot(chosen, fitted[...], preferred_element_type=F32)
        for t in range(3):
            ref[k, t] = picked[GROUP * t : GROUP * t + GROUP].astype(BF16)

    for u in range(2):
        if u == 1:
            pl.semaphore_wait(pair_sem, 1)
        for d in range(6):
            pick(chunk_of(d, core ^ u), asend, u * 6 + d)
            a_copy(d, u).start()
    for h in range(2):
        pick((colour * 2 + 1 - core) * 2 + h, asend, 12 + h)
        a_sib(h).start()
    send_tracks(1)
    pl.semaphore_wait(plane_sem, 3)
    tell(all_sem, 0)
    for h in range(2):
        for t in range(3):
            gather((colour * 2 + 1 - core) * 2 + h, t, gsend, 12 + h)
            g_sib(h, t).start()
    for h in range(2):
        pick((colour * 2 + core) * 2 + h, arecv, 12 + 2 * core + h)
        for t in range(3):
            gather((colour * 2 + core) * 2 + h, t, grecv, 12 + 2 * core + h)

    v_acc[...] = jnp.zeros_like(v_acc)

    lane = lax.broadcasted_iota(jnp.int32, (GROUP, 128), 1)
    track = lax.broadcasted_iota(jnp.int32, (GROUP, 128), 0)
    residue = track % 4
    blocks = [(lane // HITS + 4 * v) == track for v in range(2)]
    subf = lax.broadcasted_iota(jnp.int32, (GROUP, 256), 0).astype(F32)

    def group_of(m, q):
        far = m - 2
        source = jnp.where(m == 0, core, 1 - core)
        k = jnp.where(m < 2, 12 + 2 * source + q // 3, far // 3 * 6 + q)
        return k, jnp.where(m < 2, q % 3, far % 3)

    def batch(m, carry):
        found = [group_of(m, q) for q in range(6)]

        @pl.when(m >= 1)
        def _():
            for k, t in found:
                pltpu.make_async_remote_copy(
                    src_ref=gsend.at[0, 0], dst_ref=grecv.at[k, t], send_sem=gs_sem.at[0, 0],
                    recv_sem=gr_sem.at[k, t], device_id=sibling).wait_recv()

        def aux_arrival(k):
            pltpu.make_async_remote_copy(
                src_ref=asend.at[0], dst_ref=arecv.at[k], send_sem=as_sem.at[0],
                recv_sem=ar_sem.at[k], device_id=sibling).wait_recv()

        @pl.when(m == 1)
        def _():
            for h in range(2):
                aux_arrival(12 + 2 * (1 - core) + h)

        @pl.when(jnp.logical_and(m >= 2, (m - 2) % 3 == 0))
        def _():
            for d in range(6):
                aux_arrival((m - 2) // 3 * 6 + d)

        parts, wps = [], []
        vec = None
        for k, t in found:
            aj = arecv[k, t].astype(F32)
            gj = grecv[k, t].reshape(GROUP * HITS, BS)
            turned = []
            for v in range(2):
                half = aj[:, 128 * v : 128 * v + 128]
                turned.append([half] + [pltpu.roll(half, HITS * k, 1) for k in range(1, 4)])

            def spread_lanes(q):
                options = turned[q // 4]
                own_turn = options[(3 - q) % 4]
                for k in range(3):
                    own_turn = jnp.where(residue == k, options[(k - q) % 4], own_turn)
                return jnp.concatenate([jnp.where(b, own_turn, 0.0) for b in blocks], axis=1)

            place = spread_lanes(7)
            base = [spread_lanes(q) for q in range(5)]
            rows = []
            for p in range(BR):
                here = place == float(p)
                rows.extend(jnp.where(here, b, 0.0) for b in base)
            left = jnp.concatenate(rows, axis=0).astype(BF16)
            parts.append(jnp.dot(left, gj, preferred_element_type=F32))
            prow = jnp.sum(place, axis=0, keepdims=True)
            hrow = jnp.sum(spread_lanes(5), axis=0, keepdims=True)
            wrow = jnp.sum(spread_lanes(6), axis=0, keepdims=True)
            onp = subf == prow
            vj = jnp.dot(jnp.where(onp, hrow, 0.0).astype(BF16), gj, preferred_element_type=F32)
            vec = vj if vec is None else vec + vj
            wps.append(jnp.where(onp, wrow, 0.0).astype(BF16))
        v_acc[...] += vec
        for h in range(2):
            wp_buf[2 * m + h] = jnp.concatenate(wps[3 * h : 3 * h + 3], axis=1)
        rows = pl.ds(pl.multiple_of(m * 240, 16), 240)
        for p in range(BR):
            piece = jnp.concatenate([q[40 * p : 40 * p + 40] for q in parts], axis=0).astype(BF16)
            s_buf[rows, BS * p : BS * p + BS] = piece
            if p < 4:
                s_buf[rows, WIDTH + BS * p : WIDTH + BS * p + BS] = piece
        return carry

    def product(yy, first, count):
        start = pl.multiple_of(yy * 256, 256)
        return lax.dot_general(
            s_buf[first : first + count, pl.ds(start, 256)], s_buf[first : first + count, pl.ds(start, 768)],
            (((0,), (0,)), ((), ())), preferred_element_type=F32)

    def accumulate(first, count):
        def body(yy, carry):
            p = product(yy, first, count)
            p_acc[yy] = p if first == 0 else p_acc[yy] + p
            return carry
        lax.fori_loop(0, 4, body, 0)

    lax.fori_loop(0, 2, batch, 0)
    accumulate(0, 480)
    lax.fori_loop(2, 5, batch, 0)
    accumulate(480, 720)
    lax.fori_loop(5, 8, batch, 0)
    pl.semaphore_wait(all_sem, 3)

    def target(i):
        return {"region": colour * 2 + core, "tile": i}

    def p_copy(i, count):
        return pltpu.make_async_remote_copy(
            src_ref=psend.at[i, pl.ds(0, count)], dst_ref=precv.at[tile, pl.ds(0, count)],
            send_sem=ps_sem.at[i], recv_sem=pr_sem.at[tile], device_id=target(i))

    def v_copy(i):
        return pltpu.make_async_remote_copy(
            src_ref=vsend.at[i // 2], dst_ref=vrecv.at[tile],
            send_sem=vs_sem.at[i], recv_sem=vr_sem.at[tile], device_id=target(i))

    def d_copy(i):
        return pltpu.make_async_remote_copy(
            src_ref=dsend.at[i], dst_ref=drecv.at[tile],
            send_sem=ds_sem.at[i], recv_sem=dr_sem.at[tile], device_id=target(i))

    def is_self(i):
        return jnp.logical_and(own_worker, i == tile)

    for p in range(BR):
        vsend[p] = v_acc[p : p + 1, :]

    def turn(s):
        return jnp.where(s == 0, 1, jnp.where(s == 1, 3, jnp.where(s == 2, 2, 0)))

    def piece(s, carry):
        yy = (y + turn(s)) % 4
        prod = p_acc[yy] + product(yy, 1200, 720)
        for e in range(2):
            part = -prod[128 * e : 128 * e + 128, 128 * e : 128 * e + 640]
            d_acc[pl.ds(pl.multiple_of(yy * 256 + 128 * e, 128), 128), :] = part[:, :128]
            part = part.astype(BF16)
            for u in range(2):
                for j in range(4):
                    psend[yy * 4 + e * 2 + u, j] = part[ROWS * u : ROWS * u + ROWS, BS * (j + 1) : BS * (j + 2)]
        for u in (1, 3, 2, 0):
            i = yy * 4 + (x + u) % 4
            other = jnp.logical_not(is_self(i))

            @pl.when(jnp.logical_and(other, yy < 2))
            def _():
                p_copy(i, 4).start()

            @pl.when(jnp.logical_and(other, yy >= 2))
            def _():
                p_copy(i, 3).start()

            @pl.when(other)
            def _():
                v_copy(i).start()

            @pl.when(is_self(i))
            def _():
                precv[tile] = psend[i]
                vrecv[tile] = vsend[i // 2]
        return carry

    lax.fori_loop(0, 4, piece, 0)

    def diagonal(m, carry):
        found = [group_of(m // 2, m % 2 * 3 + q) for q in range(3)]
        g = jnp.concatenate([grecv[k, t].reshape(GROUP * HITS, BS) for k, t in found], axis=0)
        gt = jnp.transpose(g)
        wp = wp_buf[m]
        for p in range(BR):
            lhs[BS * p : BS * p + BS, :] = gt * wp[p : p + 1, :]
        d_acc[...] += jnp.dot(lhs[...], g, preferred_element_type=F32)
        return carry

    lax.fori_loop(0, CHUNKS, diagonal, 0)

    def send_diagonal(s, carry):
        i = (y + turn(s // 4)) % 4 * 4 + (x + turn(s % 4)) % 4
        dsend[i] = d_acc[pl.ds(pl.multiple_of(i * ROWS, ROWS), ROWS), :].astype(BF16)

        @pl.when(jnp.logical_not(is_self(i)))
        def _():
            d_copy(i).start()

        @pl.when(is_self(i))
        def _():
            drecv[tile] = dsend[i]
        return carry

    lax.fori_loop(0, 16, send_diagonal, 0)

    def p_arrival(i, count):
        return pltpu.make_async_remote_copy(
            src_ref=psend.at[0, pl.ds(0, count)], dst_ref=precv.at[i, pl.ds(0, count)],
            send_sem=ps_sem.at[0], recv_sem=pr_sem.at[i], device_id=sibling)

    def collect(i, carry):
        other = jnp.logical_not(is_self(i))

        @pl.when(jnp.logical_and(other, mine < 4))
        def _():
            p_arrival(i, 4).wait_recv()

        @pl.when(jnp.logical_and(other, mine >= 4))
        def _():
            p_arrival(i, 3).wait_recv()

        @pl.when(other)
        def _():
            pltpu.make_async_remote_copy(
                src_ref=vsend.at[0], dst_ref=vrecv.at[i], send_sem=vs_sem.at[0],
                recv_sem=vr_sem.at[i], device_id=sibling).wait_recv()
        return carry

    lax.fori_loop(0, 16, collect, 0)

    def x_copy(j, e):
        k = 2 * j - 2 + e
        return pltpu.make_async_remote_copy(
            src_ref=xsend.at[k], dst_ref=xrecv.at[2 * j - 2 + tile % 2],
            send_sem=xs_sem.at[k], recv_sem=xr_sem.at[2 * j - 2 + tile % 2], device_id=owner(mine + j, e))

    def x_arrival(j, e):
        k = 2 * j - 2 + e
        return pltpu.make_async_remote_copy(
            src_ref=xsend.at[k], dst_ref=xrecv.at[k],
            send_sem=xs_sem.at[k], recv_sem=xr_sem.at[k], device_id=sibling)

    def column(b):
        return pl.ds(pl.multiple_of(((b + 8) % 8) * BS, BS), BS)

    def reduce_block(j):
        total = precv[0, j - 1].astype(F32)
        for i in range(1, 16):
            total = total + precv[i, j - 1].astype(F32)
        out_ref[0, :, column(mine + j)] = total
        turned = jnp.transpose(total)
        for e in range(2):
            t = turned[ROWS * e : ROWS * e + ROWS]
            xsend[2 * j - 2 + e] = jnp.concatenate([t[:32], t[32:]], axis=1).astype(BF16)
            x_copy(j, e).start()

    def receive_block(j):
        for e in range(2):
            x_arrival(j, e).wait_recv()
        q0, q1 = xrecv[2 * j - 2].astype(F32), xrecv[2 * j - 1].astype(F32)
        out_ref[0, 0:32, column(mine - j)] = jnp.concatenate([q0[:, :ROWS], q1[:, :ROWS]], axis=1)
        out_ref[0, 32:64, column(mine - j)] = jnp.concatenate([q0[:, ROWS:], q1[:, ROWS:]], axis=1)

    @pl.when(mine < 4)
    def _():
        reduce_block(4)

    for j in range(3, 0, -1):
        reduce_block(j)

    row = vrecv[0]
    for i in range(1, 16):
        row = row + vrecv[i]
    vec_ref[...] = jnp.where(tile % 2 == 0, row[:, :ROWS], row[:, ROWS:])

    def collect_diagonal(i, carry):
        @pl.when(jnp.logical_not(is_self(i)))
        def _():
            pltpu.make_async_remote_copy(
                src_ref=dsend.at[0], dst_ref=drecv.at[i], send_sem=ds_sem.at[0],
                recv_sem=dr_sem.at[i], device_id=sibling).wait_recv()
        return carry

    lax.fori_loop(0, 16, collect_diagonal, 0)
    total = drecv[0].astype(F32)
    for i in range(1, 16):
        total = total + drecv[i].astype(F32)
    out_ref[0, :, column(mine)] = total

    for j in range(1, 4):
        receive_block(j)

    @pl.when(mine >= 4)
    def _():
        receive_block(4)

    for j in range(1, 4):
        for e in range(2):
            x_copy(j, e).wait_send()

    @pl.when(mine < 4)
    def _():
        for e in range(2):
            x_copy(4, e).wait_send()

    for u in range(2):
        for d in range(6):
            for t in range(3):
                g_copy(d, u, t).wait_send()
            a_copy(d, u).wait_send()
    for h in range(2):
        for t in range(3):
            g_sib(h, t).wait_send()
        a_sib(h).wait_send()

    def finish(i, carry):
        other = jnp.logical_not(is_self(i))

        @pl.when(jnp.logical_and(other, i < 8))
        def _():
            p_copy(i, 4).wait_send()

        @pl.when(jnp.logical_and(other, i >= 8))
        def _():
            p_copy(i, 3).wait_send()

        @pl.when(other)
        def _():
            v_copy(i).wait_send()
            d_copy(i).wait_send()
        return carry

    lax.fori_loop(0, 16, finish, 0)


def hand_over(matrix_ref, vector_ref, out_ref, vec_ref):
    out_ref[...] = matrix_ref[...]
    vec_ref[...] = vector_ref[...]


def local(
    global_deriv,
    local_deriv,
    hit_weight,
    hit_resid,
    block_ids,
    hit_count,
    track_region,
    block_place,
):
    vmem = pl.BlockSpec(memory_space=pltpu.VMEM)
    dma = pltpu.SemaphoreType.DMA
    matrix, vector = pl.pallas_call(
        kernel,
        name="assemble",
        out_shape=(
            jax.ShapeDtypeStruct((1, ROWS, WIDTH), F32),
            jax.ShapeDtypeStruct((1, ROWS), F32),
        ),
        in_specs=[pl.BlockSpec(memory_space=pltpu.SMEM)] + [vmem] * 7,
        out_specs=(vmem, vmem),
        scratch_shapes=[
            pltpu.SMEM((1, N_REGION * CAP), jnp.int32),
            pltpu.VMEM((BR, N_REGION * CAP), jnp.int32),
            pltpu.VMEM((14, 3, GROUP, HITS, BS), BF16),
            pltpu.VMEM((CHUNKS, 3, GROUP, HITS, BS), BF16),
            pltpu.VMEM((14, 3, GROUP, 256), BF16),
            pltpu.VMEM((CHUNKS, 3, GROUP, 256), BF16),
            pltpu.VMEM((TRK, 256), BF16),
            pltpu.VMEM((WIDTH, HALF * HITS), BF16),
            pltpu.VMEM((CHUNKS, BR, HALF * HITS), BF16),
            pltpu.VMEM((CHUNKS * 120, WIDTH + WIDTH // 2), BF16),
            pltpu.VMEM((4, 256, 768), F32),
            pltpu.VMEM((WIDTH, BS), F32),
            pltpu.VMEM((BR, BS), F32),
            pltpu.VMEM((BR, 1, BS), F32),
            pltpu.VMEM((16, 4, ROWS, BS), BF16),
            pltpu.VMEM((16, 4, ROWS, BS), BF16),
            pltpu.VMEM((16, 1, BS), F32),
            pltpu.VMEM((16, ROWS, BS), BF16),
            pltpu.VMEM((16, ROWS, BS), BF16),
            pltpu.VMEM((8, 32, BS), BF16),
            pltpu.VMEM((8, 32, BS), BF16),
            dma((14, 3)), dma((16, 3)), dma((14,)), dma((16,)),
            dma((16,)), dma((16,)), dma((16,)), dma((16,)), dma((16,)), dma((16,)), dma((8,)), dma((8,)), dma,
            pltpu.SemaphoreType.REGULAR, pltpu.SemaphoreType.REGULAR, pltpu.SemaphoreType.REGULAR,
        ],
        compiler_params=pltpu.CompilerParams(
            collective_id=0, has_side_effects=True, vmem_limit_bytes=56 << 20),
    )(
        block_place, global_deriv, local_deriv.transpose(1, 2, 0), hit_weight.T, hit_resid.T,
        block_ids.T, hit_count.reshape(1, TRK), track_region.reshape(1, TRK))
    return pl.pallas_call(
        hand_over,
        name="hand_over",
        out_shape=(
            jax.ShapeDtypeStruct((1, ROWS, WIDTH), F32),
            jax.ShapeDtypeStruct((1, ROWS), F32),
        ),
        in_specs=[vmem, vmem],
        out_specs=(vmem, vmem),
    )(matrix, vector)


def solution(mesh):
    return jax.shard_map(
        local,
        mesh=mesh,
        in_specs=(
            P(("region", "tile"), None, None),
            P(("region", "tile"), None, None),
            P(("region", "tile"), None),
            P(("region", "tile"), None),
            P(("region", "tile"), None),
            P(("region", "tile")),
            P(("region", "tile"), None),
            P(),
        ),
        out_specs=(P("region", "tile", None), P("region", "tile")),
        check_vma=False,
    )
```

```python
import functools

import jax
import jax.numpy as jnp
from jax import lax
from jax.experimental import pallas as pl
from jax.experimental.pallas import tpu as pltpu
from jax.sharding import PartitionSpec as P

BS = 128
BR = 8
HITS = 32
TRK = 192
CAP = 48
N_REGION = 8
HALF = CAP // 2
GROUP = 8
CHUNKS = 16
ROWS = 64
WIDTH = BR * BS
F32 = jnp.float32
BF16 = jnp.bfloat16
DIRS = (
    (1, 0, 0, 1, 0),
    (0, 0, 1, 1, 1),
    (-1, 0, 0, 3, 0),
    (0, 0, -1, 3, 1),
    (0, 1, 0, 2, 0),
    (0, -1, 0, 2, 1),
)


def fit(slopes, w, r, place):
    wl = [s * w for s in slopes]
    gamma = [[None] * 5 for _ in range(5)]
    for a in range(5):
        for b in range(a + 1):
            gamma[a][b] = jnp.sum(wl[a] * slopes[b], axis=0, keepdims=True) + (1.0 if a == b else 0.0)
    beta = [jnp.sum(wl[a] * r, axis=0, keepdims=True) for a in range(5)]
    factor = [[None] * 5 for _ in range(5)]
    inverse = [None] * 5
    for j in range(5):
        center = gamma[j][j]
        for k in range(j):
            center = center - factor[j][k] * factor[j][k]
        factor[j][j] = jnp.sqrt(center)
        inverse[j] = 1.0 / factor[j][j]
        for i in range(j + 1, 5):
            off = gamma[i][j]
            for k in range(j):
                off = off - factor[i][k] * factor[j][k]
            factor[i][j] = off * inverse[j]
    solved, target = [], []
    for j in range(5):
        cur, tgt = wl[j], beta[j]
        for k in range(j):
            cur = cur - factor[j][k] * solved[k]
            tgt = tgt - factor[j][k] * target[k]
        solved.append(cur * inverse[j])
        target.append(tgt * inverse[j])
    hit = w * r
    for k in range(5):
        hit = hit - solved[k] * target[k]
    full = jnp.concatenate(solved + [hit, w, place], axis=0)
    return jnp.transpose(full).astype(BF16)


def kernel(
    place_ref, g_ref, slope_ref, weight_ref, resid_ref, block_ref, count_ref, region_ref,
    out_ref, vec_ref, idx_ref, idx_vec,
    gsend, grecv, asend, arecv, fitted, lhs, wp_buf, s_buf, p_acc, d_acc, v_acc, vsend,
    psend, precv, vrecv, dsend, drecv, xsend, xrecv,
    gs_sem, gr_sem, as_sem, ar_sem, ps_sem, pr_sem, vs_sem, vr_sem, ds_sem, dr_sem, xs_sem, xr_sem, idx_sem, pair_sem, plane_sem, all_sem,
):
    region = lax.axis_index("region")
    tile = lax.axis_index("tile")
    z, core = region // 2, region % 2
    y, x = tile // 4, tile % 4
    colour = (x + 2 * y + z) % 4

    def device(nx, ny, nz, ncore):
        return {"region": nz * 2 + ncore, "tile": ny * 4 + nx}

    def neighbour(d, ncore):
        dx, dy, dz = DIRS[d][:3]
        return device((x + dx + 4) % 4, (y + dy + 4) % 4, (z + dz + 4) % 4, ncore)

    sibling = device(x, y, z, 1 - core)

    barrier = pltpu.get_barrier_semaphore()
    for d in range(6):
        pl.semaphore_signal(barrier, inc=1, device_id=neighbour(d, core))
    pl.semaphore_signal(barrier, inc=1, device_id=sibling)

    def along(axis, k):
        steps = [k if axis == n else 0 for n in range(3)]
        return device((x + steps[0]) % 4, (y + steps[1]) % 4, (z + steps[2]) % 4, core)

    for axis in range(3):
        pl.semaphore_signal(barrier, inc=1, device_id=along(axis, 2))

    own_worker = (x + 2 * y) % 4 == 0
    mine = tile // 2

    def owner(a, e):
        return {"region": region, "tile": ((a + 8) % 8) * 2 + e}

    def tell(sem, axis):
        for k in range(1, 4):
            pl.semaphore_signal(sem, inc=1, device_id=along(axis, k))

    reg = region_ref[...]
    tracks8 = lax.broadcasted_iota(jnp.int32, (BR, TRK), 0)
    named = jnp.where(reg == tracks8, 1.0, 0.0)
    earlier = (
        lax.broadcasted_iota(jnp.int32, (TRK, TRK), 0) < lax.broadcasted_iota(jnp.int32, (TRK, TRK), 1))
    ahead = jnp.dot(named.astype(BF16), jnp.where(earlier, 1.0, 0.0).astype(BF16), preferred_element_type=F32)
    slot = reg.astype(F32) * CAP + jnp.sum(named * ahead, axis=0, keepdims=True)
    slot_col = jnp.transpose(jnp.broadcast_to(slot, (BR, TRK)))[:, 0:1]
    slot_lane = lax.broadcasted_iota(jnp.int32, (TRK, N_REGION * CAP), 1).astype(F32)
    onehot = jnp.where(slot_col == slot_lane, 1.0, 0.0).astype(BF16)
    number = lax.broadcasted_iota(jnp.int32, (BR, TRK), 1).astype(F32).astype(BF16)
    idx_vec[...] = jnp.dot(number, onehot, preferred_element_type=F32).astype(jnp.int32)
    idx_copy = pltpu.make_async_copy(idx_vec.at[pl.ds(0, 1)], idx_ref, idx_sem)
    idx_copy.start()
    idx_copy.wait()

    def gather(q, t, ref, k):
        for i in range(GROUP):
            ref[k, t, i] = g_ref[jnp.clip(idx_ref[0, q * HALF + t * GROUP + i], 0, TRK - 1)]

    def chunk_of(d, c):
        step, half = DIRS[d][3:]
        return (((colour + step) % 4) * 2 + c) * 2 + half

    def g_copy(d, u, t):
        k = u * 6 + d
        return pltpu.make_async_remote_copy(
            src_ref=gsend.at[k, t], dst_ref=grecv.at[k, t],
            send_sem=gs_sem.at[k, t], recv_sem=gr_sem.at[k, t],
            device_id=neighbour(d, core ^ u))

    def a_copy(d, u):
        k = u * 6 + d
        return pltpu.make_async_remote_copy(
            src_ref=asend.at[k], dst_ref=arecv.at[k],
            send_sem=as_sem.at[k], recv_sem=ar_sem.at[k],
            device_id=neighbour(d, core ^ u))

    def g_sib(h, t):
        return pltpu.make_async_remote_copy(
            src_ref=gsend.at[12 + h, t], dst_ref=grecv.at[12 + 2 * core + h, t],
            send_sem=gs_sem.at[12 + h, t], recv_sem=gr_sem.at[12 + 2 * core + h, t],
            device_id=sibling)

    def a_sib(h):
        return pltpu.make_async_remote_copy(
            src_ref=asend.at[12 + h], dst_ref=arecv.at[12 + 2 * core + h],
            send_sem=as_sem.at[12 + h], recv_sem=ar_sem.at[12 + 2 * core + h],
            device_id=sibling)

    def send_tracks(u):
        for t in range(3):
            for d in range(6):
                gather(chunk_of(d, core ^ u), t, gsend, u * 6 + d)
                if u == 0 and t == 0 and d == 0:
                    pl.semaphore_wait(barrier, 10)
                g_copy(d, u, t).start()

    send_tracks(0)
    pl.semaphore_signal(pair_sem, inc=1, device_id=sibling)
    tell(plane_sem, 1)

    live = lax.broadcasted_iota(jnp.int32, (HITS, TRK), 0) < count_ref[...]
    weight = jnp.where(live, weight_ref[...].astype(F32), 0.0)
    ids = block_ref[...]
    place = jnp.zeros((HITS, TRK), F32)
    for b in range(BR):
        place = jnp.where(ids == b, place_ref[b].astype(F32), place)
    fitted[...] = fit(
        [slope_ref[c].astype(F32) for c in range(5)], weight, resid_ref[...].astype(F32), place)

    def pick(q, ref, k):
        rows = (q * HALF + lax.broadcasted_iota(jnp.int32, (HALF, TRK), 0)).astype(F32)
        chosen = jnp.where(slot == rows, 1.0, 0.0).astype(BF16)
        picked = jnp.dot(chosen, fitted[...], preferred_element_type=F32)
        for t in range(3):
            ref[k, t] = picked[GROUP * t : GROUP * t + GROUP].astype(BF16)

    for u in range(2):
        if u == 1:
            pl.semaphore_wait(pair_sem, 1)
        for d in range(6):
            pick(chunk_of(d, core ^ u), asend, u * 6 + d)
            a_copy(d, u).start()
    for h in range(2):
        pick((colour * 2 + 1 - core) * 2 + h, asend, 12 + h)
        a_sib(h).start()
    send_tracks(1)
    pl.semaphore_wait(plane_sem, 3)
    tell(all_sem, 0)
    for h in range(2):
        for t in range(3):
            gather((colour * 2 + 1 - core) * 2 + h, t, gsend, 12 + h)
            g_sib(h, t).start()
    for h in range(2):
        pick((colour * 2 + core) * 2 + h, arecv, 12 + 2 * core + h)
        for t in range(3):
            gather((colour * 2 + core) * 2 + h, t, grecv, 12 + 2 * core + h)

    v_acc[...] = jnp.zeros_like(v_acc)

    lane = lax.broadcasted_iota(jnp.int32, (GROUP, 128), 1)
    track = lax.broadcasted_iota(jnp.int32, (GROUP, 128), 0)
    residue = track % 4
    blocks = [(lane // HITS + 4 * v) == track for v in range(2)]
    subf = lax.broadcasted_iota(jnp.int32, (GROUP, 256), 0).astype(F32)

    def group_of(m, q):
        far = m - 2
        source = jnp.where(m == 0, core, 1 - core)
        k = jnp.where(m < 2, 12 + 2 * source + q // 3, far // 3 * 6 + q)
        return k, jnp.where(m < 2, q % 3, far % 3)

    def batch(m, carry):
        found = [group_of(m, q) for q in range(6)]

        @pl.when(m >= 1)
        def _():
            for k, t in found:
                pltpu.make_async_remote_copy(
                    src_ref=gsend.at[0, 0], dst_ref=grecv.at[k, t], send_sem=gs_sem.at[0, 0],
                    recv_sem=gr_sem.at[k, t], device_id=sibling).wait_recv()

        def aux_arrival(k):
            pltpu.make_async_remote_copy(
                src_ref=asend.at[0], dst_ref=arecv.at[k], send_sem=as_sem.at[0],
                recv_sem=ar_sem.at[k], device_id=sibling).wait_recv()

        @pl.when(m == 1)
        def _():
            for h in range(2):
                aux_arrival(12 + 2 * (1 - core) + h)

        @pl.when(jnp.logical_and(m >= 2, (m - 2) % 3 == 0))
        def _():
            for d in range(6):
                aux_arrival((m - 2) // 3 * 6 + d)

        parts, wps = [], []
        vec = None
        for k, t in found:
            aj = arecv[k, t].astype(F32)
            gj = grecv[k, t].reshape(GROUP * HITS, BS)
            turned = []
            for v in range(2):
                half = aj[:, 128 * v : 128 * v + 128]
                turned.append([half] + [pltpu.roll(half, HITS * k, 1) for k in range(1, 4)])

            def spread_lanes(q):
                options = turned[q // 4]
                own_turn = options[(3 - q) % 4]
                for k in range(3):
                    own_turn = jnp.where(residue == k, options[(k - q) % 4], own_turn)
                return jnp.concatenate([jnp.where(b, own_turn, 0.0) for b in blocks], axis=1)

            place = spread_lanes(7)
            base = [spread_lanes(q) for q in range(5)]
            rows = []
            for p in range(BR):
                here = place == float(p)
                rows.extend(jnp.where(here, b, 0.0) for b in base)
            left = jnp.concatenate(rows, axis=0).astype(BF16)
            parts.append(jnp.dot(left, gj, preferred_element_type=F32))
            prow = jnp.sum(place, axis=0, keepdims=True)
            hrow = jnp.sum(spread_lanes(5), axis=0, keepdims=True)
            wrow = jnp.sum(spread_lanes(6), axis=0, keepdims=True)
            onp = subf == prow
            vj = jnp.dot(jnp.where(onp, hrow, 0.0).astype(BF16), gj, preferred_element_type=F32)
            vec = vj if vec is None else vec + vj
            wps.append(jnp.where(onp, wrow, 0.0).astype(BF16))
        v_acc[...] += vec
        for h in range(2):
            wp_buf[2 * m + h] = jnp.concatenate(wps[3 * h : 3 * h + 3], axis=1)
        rows = pl.ds(pl.multiple_of(m * 240, 16), 240)
        for p in range(BR):
            piece = jnp.concatenate([q[40 * p : 40 * p + 40] for q in parts], axis=0).astype(BF16)
            s_buf[rows, BS * p : BS * p + BS] = piece
            if p < 4:
                s_buf[rows, WIDTH + BS * p : WIDTH + BS * p + BS] = piece
        return carry

    def product(yy, first, count):
        start = pl.multiple_of(yy * 256, 256)
        return lax.dot_general(
            s_buf[first : first + count, pl.ds(start, 256)], s_buf[first : first + count, pl.ds(start, 768)],
            (((0,), (0,)), ((), ())), preferred_element_type=F32)

    def accumulate(first, count):
        def body(yy, carry):
            p = product(yy, first, count)
            p_acc[yy] = p if first == 0 else p_acc[yy] + p
            return carry
        lax.fori_loop(0, 4, body, 0)

    def step(m, carry):
        batch(m, carry)

        @pl.when(m == 1)
        def _():
            accumulate(0, 480)

        @pl.when(m == 4)
        def _():
            accumulate(480, 720)
        return carry

    lax.fori_loop(0, 8, step, 0)
    pl.semaphore_wait(all_sem, 3)

    def target(i):
        return {"region": colour * 2 + core, "tile": i}

    def p_copy(i, count):
        return pltpu.make_async_remote_copy(
            src_ref=psend.at[i, pl.ds(0, count)], dst_ref=precv.at[tile, pl.ds(0, count)],
            send_sem=ps_sem.at[i], recv_sem=pr_sem.at[tile], device_id=target(i))

    def v_copy(i):
        return pltpu.make_async_remote_copy(
            src_ref=vsend.at[i // 2], dst_ref=vrecv.at[tile],
            send_sem=vs_sem.at[i], recv_sem=vr_sem.at[tile], device_id=target(i))

    def d_copy(i):
        return pltpu.make_async_remote_copy(
            src_ref=dsend.at[i], dst_ref=drecv.at[tile],
            send_sem=ds_sem.at[i], recv_sem=dr_sem.at[tile], device_id=target(i))

    def is_self(i):
        return jnp.logical_and(own_worker, i == tile)

    for p in range(BR):
        vsend[p] = v_acc[p : p + 1, :]

    def turn(s):
        return jnp.where(s == 0, 1, jnp.where(s == 1, 3, jnp.where(s == 2, 2, 0)))

    def piece(s, carry):
        yy = (y + turn(s)) % 4
        prod = p_acc[yy] + product(yy, 1200, 720)
        for e in range(2):
            part = -prod[128 * e : 128 * e + 128, 128 * e : 128 * e + 640]
            d_acc[pl.ds(pl.multiple_of(yy * 256 + 128 * e, 128), 128), :] = part[:, :128]
            part = part.astype(BF16)
            for u in range(2):
                for j in range(4):
                    psend[yy * 4 + e * 2 + u, j] = part[ROWS * u : ROWS * u + ROWS, BS * (j + 1) : BS * (j + 2)]
        for u in (1, 3, 2, 0):
            i = yy * 4 + (x + u) % 4
            other = jnp.logical_not(is_self(i))

            @pl.when(jnp.logical_and(other, yy < 2))
            def _():
                p_copy(i, 4).start()

            @pl.when(jnp.logical_and(other, yy >= 2))
            def _():
                p_copy(i, 3).start()

            @pl.when(other)
            def _():
                v_copy(i).start()

            @pl.when(is_self(i))
            def _():
                precv[tile] = psend[i]
                vrecv[tile] = vsend[i // 2]
        return carry

    lax.fori_loop(0, 4, piece, 0)

    def diagonal(m, carry):
        found = [group_of(m // 2, m % 2 * 3 + q) for q in range(3)]
        g = jnp.concatenate([grecv[k, t].reshape(GROUP * HITS, BS) for k, t in found], axis=0)
        gt = jnp.transpose(g)
        wp = wp_buf[m]
        for p in range(BR):
            lhs[BS * p : BS * p + BS, :] = gt * wp[p : p + 1, :]
        d_acc[...] += jnp.dot(lhs[...], g, preferred_element_type=F32)
        return carry

    lax.fori_loop(0, CHUNKS, diagonal, 0)

    def send_diagonal(s, carry):
        i = (y + turn(s // 4)) % 4 * 4 + (x + turn(s % 4)) % 4
        dsend[i] = d_acc[pl.ds(pl.multiple_of(i * ROWS, ROWS), ROWS), :].astype(BF16)

        @pl.when(jnp.logical_not(is_self(i)))
        def _():
            d_copy(i).start()

        @pl.when(is_self(i))
        def _():
            drecv[tile] = dsend[i]
        return carry

    lax.fori_loop(0, 16, send_diagonal, 0)

    for u in range(2):
        for d in range(6):
            for t in range(3):
                g_copy(d, u, t).wait_send()
            a_copy(d, u).wait_send()
    for h in range(2):
        for t in range(3):
            g_sib(h, t).wait_send()
        a_sib(h).wait_send()

    def p_arrival(i, count):
        return pltpu.make_async_remote_copy(
            src_ref=psend.at[0, pl.ds(0, count)], dst_ref=precv.at[i, pl.ds(0, count)],
            send_sem=ps_sem.at[0], recv_sem=pr_sem.at[i], device_id=sibling)

    def collect(i, carry):
        other = jnp.logical_not(is_self(i))

        @pl.when(jnp.logical_and(other, mine < 4))
        def _():
            p_arrival(i, 4).wait_recv()

        @pl.when(jnp.logical_and(other, mine >= 4))
        def _():
            p_arrival(i, 3).wait_recv()

        @pl.when(other)
        def _():
            pltpu.make_async_remote_copy(
                src_ref=vsend.at[0], dst_ref=vrecv.at[i], send_sem=vs_sem.at[0],
                recv_sem=vr_sem.at[i], device_id=sibling).wait_recv()
        return carry

    lax.fori_loop(0, 16, collect, 0)

    def x_copy(j, e):
        k = 2 * j - 2 + e
        return pltpu.make_async_remote_copy(
            src_ref=xsend.at[k], dst_ref=xrecv.at[2 * j - 2 + tile % 2],
            send_sem=xs_sem.at[k], recv_sem=xr_sem.at[2 * j - 2 + tile % 2], device_id=owner(mine + j, e))

    def x_arrival(j, e):
        k = 2 * j - 2 + e
        return pltpu.make_async_remote_copy(
            src_ref=xsend.at[k], dst_ref=xrecv.at[k],
            send_sem=xs_sem.at[k], recv_sem=xr_sem.at[k], device_id=sibling)

    def column(b):
        return pl.ds(pl.multiple_of(((b + 8) % 8) * BS, BS), BS)

    def reduce_block(j):
        total = precv[0, j - 1].astype(F32)
        for i in range(1, 16):
            total = total + precv[i, j - 1].astype(F32)
        out_ref[0, :, column(mine + j)] = total
        turned = jnp.transpose(total)
        for e in range(2):
            t = turned[ROWS * e : ROWS * e + ROWS]
            xsend[2 * j - 2 + e] = jnp.concatenate([t[:32], t[32:]], axis=1).astype(BF16)
            x_copy(j, e).start()

    def receive_block(j):
        for e in range(2):
            x_arrival(j, e).wait_recv()
        q0, q1 = xrecv[2 * j - 2].astype(F32), xrecv[2 * j - 1].astype(F32)
        out_ref[0, 0:32, column(mine - j)] = jnp.concatenate([q0[:, :ROWS], q1[:, :ROWS]], axis=1)
        out_ref[0, 32:64, column(mine - j)] = jnp.concatenate([q0[:, ROWS:], q1[:, ROWS:]], axis=1)

    @pl.when(mine < 4)
    def _():
        reduce_block(4)

    for j in range(3, 0, -1):
        reduce_block(j)

    row = vrecv[0]
    for i in range(1, 16):
        row = row + vrecv[i]
    vec_ref[...] = jnp.where(tile % 2 == 0, row[:, :ROWS], row[:, ROWS:])

    def finish(i, carry):
        other = jnp.logical_not(is_self(i))

        @pl.when(jnp.logical_and(other, i < 8))
        def _():
            p_copy(i, 4).wait_send()

        @pl.when(jnp.logical_and(other, i >= 8))
        def _():
            p_copy(i, 3).wait_send()

        @pl.when(other)
        def _():
            v_copy(i).wait_send()
        return carry

    lax.fori_loop(0, 16, finish, 0)

    def collect_diagonal(i, carry):
        @pl.when(jnp.logical_not(is_self(i)))
        def _():
            pltpu.make_async_remote_copy(
                src_ref=dsend.at[0], dst_ref=drecv.at[i], send_sem=ds_sem.at[0],
                recv_sem=dr_sem.at[i], device_id=sibling).wait_recv()
        return carry

    lax.fori_loop(0, 16, collect_diagonal, 0)
    total = drecv[0].astype(F32)
    for i in range(1, 16):
        total = total + drecv[i].astype(F32)
    out_ref[0, :, column(mine)] = total

    for j in range(1, 4):
        receive_block(j)

    @pl.when(mine >= 4)
    def _():
        receive_block(4)

    for j in range(1, 4):
        for e in range(2):
            x_copy(j, e).wait_send()

    @pl.when(mine < 4)
    def _():
        for e in range(2):
            x_copy(4, e).wait_send()

    def finish_diagonal(i, carry):
        @pl.when(jnp.logical_not(is_self(i)))
        def _():
            d_copy(i).wait_send()
        return carry

    lax.fori_loop(0, 16, finish_diagonal, 0)


def hand_over(matrix_ref, vector_ref, out_ref, vec_ref):
    out_ref[...] = matrix_ref[...]
    vec_ref[...] = vector_ref[...]


def local(
    global_deriv,
    local_deriv,
    hit_weight,
    hit_resid,
    block_ids,
    hit_count,
    track_region,
    block_place,
):
    vmem = pl.BlockSpec(memory_space=pltpu.VMEM)
    dma = pltpu.SemaphoreType.DMA
    matrix, vector = pl.pallas_call(
        kernel,
        name="assemble",
        out_shape=(
            jax.ShapeDtypeStruct((1, ROWS, WIDTH), F32),
            jax.ShapeDtypeStruct((1, ROWS), F32),
        ),
        in_specs=[pl.BlockSpec(memory_space=pltpu.SMEM)] + [vmem] * 7,
        out_specs=(vmem, vmem),
        scratch_shapes=[
            pltpu.SMEM((1, N_REGION * CAP), jnp.int32),
            pltpu.VMEM((BR, N_REGION * CAP), jnp.int32),
            pltpu.VMEM((14, 3, GROUP, HITS, BS), BF16),
            pltpu.VMEM((CHUNKS, 3, GROUP, HITS, BS), BF16),
            pltpu.VMEM((14, 3, GROUP, 256), BF16),
            pltpu.VMEM((CHUNKS, 3, GROUP, 256), BF16),
            pltpu.VMEM((TRK, 256), BF16),
            pltpu.VMEM((WIDTH, HALF * HITS), BF16),
            pltpu.VMEM((CHUNKS, BR, HALF * HITS), BF16),
            pltpu.VMEM((CHUNKS * 120, WIDTH + WIDTH // 2), BF16),
            pltpu.VMEM((4, 256, 768), F32),
            pltpu.VMEM((WIDTH, BS), F32),
            pltpu.VMEM((BR, BS), F32),
            pltpu.VMEM((BR, 1, BS), F32),
            pltpu.VMEM((16, 4, ROWS, BS), BF16),
            pltpu.VMEM((16, 4, ROWS, BS), BF16),
            pltpu.VMEM((16, 1, BS), F32),
            pltpu.VMEM((16, ROWS, BS), BF16),
            pltpu.VMEM((16, ROWS, BS), BF16),
            pltpu.VMEM((8, 32, BS), BF16),
            pltpu.VMEM((8, 32, BS), BF16),
            dma((14, 3)), dma((16, 3)), dma((14,)), dma((16,)),
            dma((16,)), dma((16,)), dma((16,)), dma((16,)), dma((16,)), dma((16,)), dma((8,)), dma((8,)), dma,
            pltpu.SemaphoreType.REGULAR, pltpu.SemaphoreType.REGULAR, pltpu.SemaphoreType.REGULAR,
        ],
        compiler_params=pltpu.CompilerParams(
            collective_id=0, has_side_effects=True, vmem_limit_bytes=56 << 20),
    )(
        block_place, global_deriv, local_deriv.transpose(1, 2, 0), hit_weight.T, hit_resid.T,
        block_ids.T, hit_count.reshape(1, TRK), track_region.reshape(1, TRK))
    return pl.pallas_call(
        hand_over,
        name="hand_over",
        out_shape=(
            jax.ShapeDtypeStruct((1, ROWS, WIDTH), F32),
            jax.ShapeDtypeStruct((1, ROWS), F32),
        ),
        in_specs=[vmem, vmem],
        out_specs=(vmem, vmem),
    )(matrix, vector)


def solution(mesh):
    return jax.shard_map(
        local,
        mesh=mesh,
        in_specs=(
            P(("region", "tile"), None, None),
            P(("region", "tile"), None, None),
            P(("region", "tile"), None),
            P(("region", "tile"), None),
            P(("region", "tile"), None),
            P(("region", "tile")),
            P(("region", "tile"), None),
            P(),
        ),
        out_specs=(P("region", "tile", None), P("region", "tile")),
        check_vma=False,
    )
```

```python
import functools

import jax
import jax.numpy as jnp
from jax import lax
from jax.experimental import pallas as pl
from jax.experimental.pallas import tpu as pltpu
from jax.sharding import PartitionSpec as P

BS = 128
BR = 8
HITS = 32
TRK = 192
CAP = 48
N_REGION = 8
HALF = CAP // 2
GROUP = 8
CHUNKS = 16
ROWS = 64
WIDTH = BR * BS
F32 = jnp.float32
BF16 = jnp.bfloat16
DIRS = (
    (1, 0, 0, 1, 0),
    (0, 0, 1, 1, 1),
    (-1, 0, 0, 3, 0),
    (0, 0, -1, 3, 1),
    (0, 1, 0, 2, 0),
    (0, -1, 0, 2, 1),
)


def fit(slopes, w, r, place):
    wl = [s * w for s in slopes]
    gamma = [[None] * 5 for _ in range(5)]
    for a in range(5):
        for b in range(a + 1):
            gamma[a][b] = jnp.sum(wl[a] * slopes[b], axis=0, keepdims=True) + (1.0 if a == b else 0.0)
    beta = [jnp.sum(wl[a] * r, axis=0, keepdims=True) for a in range(5)]
    factor = [[None] * 5 for _ in range(5)]
    inverse = [None] * 5
    for j in range(5):
        center = gamma[j][j]
        for k in range(j):
            center = center - factor[j][k] * factor[j][k]
        factor[j][j] = jnp.sqrt(center)
        inverse[j] = 1.0 / factor[j][j]
        for i in range(j + 1, 5):
            off = gamma[i][j]
            for k in range(j):
                off = off - factor[i][k] * factor[j][k]
            factor[i][j] = off * inverse[j]
    solved, target = [], []
    for j in range(5):
        cur, tgt = wl[j], beta[j]
        for k in range(j):
            cur = cur - factor[j][k] * solved[k]
            tgt = tgt - factor[j][k] * target[k]
        solved.append(cur * inverse[j])
        target.append(tgt * inverse[j])
    hit = w * r
    for k in range(5):
        hit = hit - solved[k] * target[k]
    full = jnp.concatenate(solved + [hit, w, place], axis=0)
    return jnp.transpose(full).astype(BF16)


def kernel(
    place_ref, g_hbm, slope_ref, weight_ref, resid_ref, block_ref, count_ref, region_ref,
    out_ref, vec_ref, g_ref, g_sem, idx_ref, idx_vec,
    gsend, grecv, asend, arecv, fitted, lhs, wp_buf, s_buf, p_acc, d_acc, v_acc, vsend,
    psend, precv, vrecv, dsend, drecv, xsend, xrecv,
    gs_sem, gr_sem, as_sem, ar_sem, ps_sem, pr_sem, vs_sem, vr_sem, ds_sem, dr_sem, xs_sem, xr_sem, idx_sem, pair_sem, plane_sem, all_sem,
):
    region = lax.axis_index("region")
    tile = lax.axis_index("tile")
    z, core = region // 2, region % 2
    y, x = tile // 4, tile % 4
    colour = (x + 2 * y + z) % 4

    def device(nx, ny, nz, ncore):
        return {"region": nz * 2 + ncore, "tile": ny * 4 + nx}

    def neighbour(d, ncore):
        dx, dy, dz = DIRS[d][:3]
        return device((x + dx + 4) % 4, (y + dy + 4) % 4, (z + dz + 4) % 4, ncore)

    sibling = device(x, y, z, 1 - core)

    g_load = pltpu.make_async_copy(g_hbm, g_ref, g_sem)
    g_load.start()

    barrier = pltpu.get_barrier_semaphore()
    for d in range(6):
        pl.semaphore_signal(barrier, inc=1, device_id=neighbour(d, core))
    pl.semaphore_signal(barrier, inc=1, device_id=sibling)

    def along(axis, k):
        steps = [k if axis == n else 0 for n in range(3)]
        return device((x + steps[0]) % 4, (y + steps[1]) % 4, (z + steps[2]) % 4, core)

    for axis in range(3):
        pl.semaphore_signal(barrier, inc=1, device_id=along(axis, 2))

    own_worker = (x + 2 * y) % 4 == 0
    mine = tile // 2

    def owner(a, e):
        return {"region": region, "tile": ((a + 8) % 8) * 2 + e}

    def tell(sem, axis):
        for k in range(1, 4):
            pl.semaphore_signal(sem, inc=1, device_id=along(axis, k))

    reg = region_ref[...]
    tracks8 = lax.broadcasted_iota(jnp.int32, (BR, TRK), 0)
    named = jnp.where(reg == tracks8, 1.0, 0.0)
    earlier = (
        lax.broadcasted_iota(jnp.int32, (TRK, TRK), 0) < lax.broadcasted_iota(jnp.int32, (TRK, TRK), 1))
    ahead = jnp.dot(named.astype(BF16), jnp.where(earlier, 1.0, 0.0).astype(BF16), preferred_element_type=F32)
    slot = reg.astype(F32) * CAP + jnp.sum(named * ahead, axis=0, keepdims=True)
    slot_col = jnp.transpose(jnp.broadcast_to(slot, (BR, TRK)))[:, 0:1]
    slot_lane = lax.broadcasted_iota(jnp.int32, (TRK, N_REGION * CAP), 1).astype(F32)
    onehot = jnp.where(slot_col == slot_lane, 1.0, 0.0).astype(BF16)
    number = lax.broadcasted_iota(jnp.int32, (BR, TRK), 1).astype(F32).astype(BF16)
    idx_vec[...] = jnp.dot(number, onehot, preferred_element_type=F32).astype(jnp.int32)
    idx_copy = pltpu.make_async_copy(idx_vec.at[pl.ds(0, 1)], idx_ref, idx_sem)
    idx_copy.start()
    g_load.wait()
    idx_copy.wait()

    def gather(q, t, ref, k):
        for i in range(GROUP):
            ref[k, t, i] = g_ref[jnp.clip(idx_ref[0, q * HALF + t * GROUP + i], 0, TRK - 1)]

    def chunk_of(d, c):
        step, half = DIRS[d][3:]
        return (((colour + step) % 4) * 2 + c) * 2 + half

    def g_copy(d, u, t):
        k = u * 6 + d
        return pltpu.make_async_remote_copy(
            src_ref=gsend.at[k, t], dst_ref=grecv.at[k, t],
            send_sem=gs_sem.at[k, t], recv_sem=gr_sem.at[k, t],
            device_id=neighbour(d, core ^ u))

    def a_copy(d, u):
        k = u * 6 + d
        return pltpu.make_async_remote_copy(
            src_ref=asend.at[k], dst_ref=arecv.at[k],
            send_sem=as_sem.at[k], recv_sem=ar_sem.at[k],
            device_id=neighbour(d, core ^ u))

    def g_sib(h, t):
        return pltpu.make_async_remote_copy(
            src_ref=gsend.at[12 + h, t], dst_ref=grecv.at[12 + 2 * core + h, t],
            send_sem=gs_sem.at[12 + h, t], recv_sem=gr_sem.at[12 + 2 * core + h, t],
            device_id=sibling)

    def a_sib(h):
        return pltpu.make_async_remote_copy(
            src_ref=asend.at[12 + h], dst_ref=arecv.at[12 + 2 * core + h],
            send_sem=as_sem.at[12 + h], recv_sem=ar_sem.at[12 + 2 * core + h],
            device_id=sibling)

    def send_tracks(u):
        for t in range(3):
            for d in range(6):
                gather(chunk_of(d, core ^ u), t, gsend, u * 6 + d)
                if u == 0 and t == 0 and d == 0:
                    pl.semaphore_wait(barrier, 10)
                g_copy(d, u, t).start()

    send_tracks(0)
    pl.semaphore_signal(pair_sem, inc=1, device_id=sibling)
    tell(plane_sem, 1)

    live = lax.broadcasted_iota(jnp.int32, (HITS, TRK), 0) < count_ref[...]
    weight = jnp.where(live, weight_ref[...].astype(F32), 0.0)
    ids = block_ref[...]
    place = jnp.zeros((HITS, TRK), F32)
    for b in range(BR):
        place = jnp.where(ids == b, place_ref[b].astype(F32), place)
    fitted[...] = fit(
        [slope_ref[c].astype(F32) for c in range(5)], weight, resid_ref[...].astype(F32), place)

    def pick(q, ref, k):
        rows = (q * HALF + lax.broadcasted_iota(jnp.int32, (HALF, TRK), 0)).astype(F32)
        chosen = jnp.where(slot == rows, 1.0, 0.0).astype(BF16)
        picked = jnp.dot(chosen, fitted[...], preferred_element_type=F32)
        for t in range(3):
            ref[k, t] = picked[GROUP * t : GROUP * t + GROUP].astype(BF16)

    for u in range(2):
        if u == 1:
            pl.semaphore_wait(pair_sem, 1)
        for d in range(6):
            pick(chunk_of(d, core ^ u), asend, u * 6 + d)
            a_copy(d, u).start()
    for h in range(2):
        pick((colour * 2 + 1 - core) * 2 + h, asend, 12 + h)
        a_sib(h).start()
    send_tracks(1)
    pl.semaphore_wait(plane_sem, 3)
    tell(all_sem, 0)
    for h in range(2):
        for t in range(3):
            gather((colour * 2 + 1 - core) * 2 + h, t, gsend, 12 + h)
            g_sib(h, t).start()
    for h in range(2):
        pick((colour * 2 + core) * 2 + h, arecv, 12 + 2 * core + h)
        for t in range(3):
            gather((colour * 2 + core) * 2 + h, t, grecv, 12 + 2 * core + h)

    v_acc[...] = jnp.zeros_like(v_acc)

    lane = lax.broadcasted_iota(jnp.int32, (GROUP, 128), 1)
    track = lax.broadcasted_iota(jnp.int32, (GROUP, 128), 0)
    residue = track % 4
    blocks = [(lane // HITS + 4 * v) == track for v in range(2)]
    subf = lax.broadcasted_iota(jnp.int32, (GROUP, 256), 0).astype(F32)

    def group_of(m, q):
        far = m - 2
        source = jnp.where(m == 0, core, 1 - core)
        k = jnp.where(m < 2, 12 + 2 * source + q // 3, far // 3 * 6 + q)
        return k, jnp.where(m < 2, q % 3, far % 3)

    def batch(m, carry):
        found = [group_of(m, q) for q in range(6)]

        @pl.when(m >= 1)
        def _():
            for k, t in found:
                pltpu.make_async_remote_copy(
                    src_ref=gsend.at[0, 0], dst_ref=grecv.at[k, t], send_sem=gs_sem.at[0, 0],
                    recv_sem=gr_sem.at[k, t], device_id=sibling).wait_recv()

        def aux_arrival(k):
            pltpu.make_async_remote_copy(
                src_ref=asend.at[0], dst_ref=arecv.at[k], send_sem=as_sem.at[0],
                recv_sem=ar_sem.at[k], device_id=sibling).wait_recv()

        @pl.when(m == 1)
        def _():
            for h in range(2):
                aux_arrival(12 + 2 * (1 - core) + h)

        @pl.when(jnp.logical_and(m >= 2, (m - 2) % 3 == 0))
        def _():
            for d in range(6):
                aux_arrival((m - 2) // 3 * 6 + d)

        parts, wps = [], []
        vec = None
        for k, t in found:
            aj = arecv[k, t].astype(F32)
            gj = grecv[k, t].reshape(GROUP * HITS, BS)
            turned = []
            for v in range(2):
                half = aj[:, 128 * v : 128 * v + 128]
                turned.append([half] + [pltpu.roll(half, HITS * k, 1) for k in range(1, 4)])

            def spread_lanes(q):
                options = turned[q // 4]
                own_turn = options[(3 - q) % 4]
                for k in range(3):
                    own_turn = jnp.where(residue == k, options[(k - q) % 4], own_turn)
                return jnp.concatenate([jnp.where(b, own_turn, 0.0) for b in blocks], axis=1)

            place = spread_lanes(7)
            base = [spread_lanes(q) for q in range(5)]
            rows = []
            for p in range(BR):
                here = place == float(p)
                rows.extend(jnp.where(here, b, 0.0) for b in base)
            left = jnp.concatenate(rows, axis=0).astype(BF16)
            parts.append(jnp.dot(left, gj, preferred_element_type=F32))
            prow = jnp.sum(place, axis=0, keepdims=True)
            hrow = jnp.sum(spread_lanes(5), axis=0, keepdims=True)
            wrow = jnp.sum(spread_lanes(6), axis=0, keepdims=True)
            onp = subf == prow
            vj = jnp.dot(jnp.where(onp, hrow, 0.0).astype(BF16), gj, preferred_element_type=F32)
            vec = vj if vec is None else vec + vj
            wps.append(jnp.where(onp, wrow, 0.0).astype(BF16))
        v_acc[...] += vec
        for h in range(2):
            wp_buf[2 * m + h] = jnp.concatenate(wps[3 * h : 3 * h + 3], axis=1)
        rows = pl.ds(pl.multiple_of(m * 240, 16), 240)
        for p in range(BR):
            piece = jnp.concatenate([q[40 * p : 40 * p + 40] for q in parts], axis=0).astype(BF16)
            s_buf[rows, BS * p : BS * p + BS] = piece
            if p < 4:
                s_buf[rows, WIDTH + BS * p : WIDTH + BS * p + BS] = piece
        return carry

    def product(yy, first, count):
        start = pl.multiple_of(yy * 256, 256)
        return lax.dot_general(
            s_buf[first : first + count, pl.ds(start, 256)], s_buf[first : first + count, pl.ds(start, 768)],
            (((0,), (0,)), ((), ())), preferred_element_type=F32)

    def accumulate(first, count):
        def body(yy, carry):
            p = product(yy, first, count)
            p_acc[yy] = p if first == 0 else p_acc[yy] + p
            return carry
        lax.fori_loop(0, 4, body, 0)

    def step(m, carry):
        batch(m, carry)

        @pl.when(m == 1)
        def _():
            accumulate(0, 480)

        @pl.when(m == 4)
        def _():
            accumulate(480, 720)
        return carry

    lax.fori_loop(0, 8, step, 0)
    pl.semaphore_wait(all_sem, 3)

    def target(i):
        return {"region": colour * 2 + core, "tile": i}

    def p_copy(i, count):
        return pltpu.make_async_remote_copy(
            src_ref=psend.at[i, pl.ds(0, count)], dst_ref=precv.at[tile, pl.ds(0, count)],
            send_sem=ps_sem.at[i], recv_sem=pr_sem.at[tile], device_id=target(i))

    def v_copy(i):
        return pltpu.make_async_remote_copy(
            src_ref=vsend.at[i // 2], dst_ref=vrecv.at[tile],
            send_sem=vs_sem.at[i], recv_sem=vr_sem.at[tile], device_id=target(i))

    def d_copy(i):
        return pltpu.make_async_remote_copy(
            src_ref=dsend.at[i], dst_ref=drecv.at[tile],
            send_sem=ds_sem.at[i], recv_sem=dr_sem.at[tile], device_id=target(i))

    def is_self(i):
        return jnp.logical_and(own_worker, i == tile)

    for p in range(BR):
        vsend[p] = v_acc[p : p + 1, :]

    def turn(s):
        return jnp.where(s == 0, 1, jnp.where(s == 1, 3, jnp.where(s == 2, 2, 0)))

    def piece(s, carry):
        yy = (y + turn(s)) % 4
        prod = p_acc[yy] + product(yy, 1200, 720)
        for e in range(2):
            part = -prod[128 * e : 128 * e + 128, 128 * e : 128 * e + 640]
            d_acc[pl.ds(pl.multiple_of(yy * 256 + 128 * e, 128), 128), :] = part[:, :128]
            part = part.astype(BF16)
            for u in range(2):
                for j in range(4):
                    psend[yy * 4 + e * 2 + u, j] = part[ROWS * u : ROWS * u + ROWS, BS * (j + 1) : BS * (j + 2)]
        for u in (1, 3, 2, 0):
            i = yy * 4 + (x + u) % 4
            other = jnp.logical_not(is_self(i))

            @pl.when(jnp.logical_and(other, yy < 2))
            def _():
                p_copy(i, 4).start()

            @pl.when(jnp.logical_and(other, yy >= 2))
            def _():
                p_copy(i, 3).start()

            @pl.when(other)
            def _():
                v_copy(i).start()

            @pl.when(is_self(i))
            def _():
                precv[tile] = psend[i]
                vrecv[tile] = vsend[i // 2]
        return carry

    lax.fori_loop(0, 4, piece, 0)

    def diagonal(m, carry):
        found = [group_of(m // 2, m % 2 * 3 + q) for q in range(3)]
        g = jnp.concatenate([grecv[k, t].reshape(GROUP * HITS, BS) for k, t in found], axis=0)
        gt = jnp.transpose(g)
        wp = wp_buf[m]
        for p in range(BR):
            lhs[BS * p : BS * p + BS, :] = gt * wp[p : p + 1, :]
        d_acc[...] += jnp.dot(lhs[...], g, preferred_element_type=F32)
        return carry

    lax.fori_loop(0, CHUNKS, diagonal, 0)

    def send_diagonal(s, carry):
        i = (y + turn(s // 4)) % 4 * 4 + (x + turn(s % 4)) % 4
        dsend[i] = d_acc[pl.ds(pl.multiple_of(i * ROWS, ROWS), ROWS), :].astype(BF16)

        @pl.when(jnp.logical_not(is_self(i)))
        def _():
            d_copy(i).start()

        @pl.when(is_self(i))
        def _():
            drecv[tile] = dsend[i]
        return carry

    lax.fori_loop(0, 16, send_diagonal, 0)

    for u in range(2):
        for d in range(6):
            for t in range(3):
                g_copy(d, u, t).wait_send()
            a_copy(d, u).wait_send()
    for h in range(2):
        for t in range(3):
            g_sib(h, t).wait_send()
        a_sib(h).wait_send()

    def p_arrival(i, count):
        return pltpu.make_async_remote_copy(
            src_ref=psend.at[0, pl.ds(0, count)], dst_ref=precv.at[i, pl.ds(0, count)],
            send_sem=ps_sem.at[0], recv_sem=pr_sem.at[i], device_id=sibling)

    def collect(i, carry):
        other = jnp.logical_not(is_self(i))

        @pl.when(jnp.logical_and(other, mine < 4))
        def _():
            p_arrival(i, 4).wait_recv()

        @pl.when(jnp.logical_and(other, mine >= 4))
        def _():
            p_arrival(i, 3).wait_recv()

        @pl.when(other)
        def _():
            pltpu.make_async_remote_copy(
                src_ref=vsend.at[0], dst_ref=vrecv.at[i], send_sem=vs_sem.at[0],
                recv_sem=vr_sem.at[i], device_id=sibling).wait_recv()
        return carry

    lax.fori_loop(0, 16, collect, 0)

    def x_copy(j, e):
        k = 2 * j - 2 + e
        return pltpu.make_async_remote_copy(
            src_ref=xsend.at[k], dst_ref=xrecv.at[2 * j - 2 + tile % 2],
            send_sem=xs_sem.at[k], recv_sem=xr_sem.at[2 * j - 2 + tile % 2], device_id=owner(mine + j, e))

    def x_arrival(j, e):
        k = 2 * j - 2 + e
        return pltpu.make_async_remote_copy(
            src_ref=xsend.at[k], dst_ref=xrecv.at[k],
            send_sem=xs_sem.at[k], recv_sem=xr_sem.at[k], device_id=sibling)

    def column(b):
        return pl.ds(pl.multiple_of(((b + 8) % 8) * BS, BS), BS)

    def reduce_block(j):
        total = precv[0, j - 1].astype(F32)
        for i in range(1, 16):
            total = total + precv[i, j - 1].astype(F32)
        out_ref[0, :, column(mine + j)] = total
        turned = jnp.transpose(total)
        for e in range(2):
            t = turned[ROWS * e : ROWS * e + ROWS]
            xsend[2 * j - 2 + e] = jnp.concatenate([t[:32], t[32:]], axis=1).astype(BF16)
            x_copy(j, e).start()

    def receive_block(j):
        for e in range(2):
            x_arrival(j, e).wait_recv()
        q0, q1 = xrecv[2 * j - 2].astype(F32), xrecv[2 * j - 1].astype(F32)
        out_ref[0, 0:32, column(mine - j)] = jnp.concatenate([q0[:, :ROWS], q1[:, :ROWS]], axis=1)
        out_ref[0, 32:64, column(mine - j)] = jnp.concatenate([q0[:, ROWS:], q1[:, ROWS:]], axis=1)

    @pl.when(mine < 4)
    def _():
        reduce_block(4)

    for j in range(3, 0, -1):
        reduce_block(j)

    row = vrecv[0]
    for i in range(1, 16):
        row = row + vrecv[i]
    vec_ref[...] = jnp.where(tile % 2 == 0, row[:, :ROWS], row[:, ROWS:])

    def finish(i, carry):
        other = jnp.logical_not(is_self(i))

        @pl.when(jnp.logical_and(other, i < 8))
        def _():
            p_copy(i, 4).wait_send()

        @pl.when(jnp.logical_and(other, i >= 8))
        def _():
            p_copy(i, 3).wait_send()

        @pl.when(other)
        def _():
            v_copy(i).wait_send()
        return carry

    lax.fori_loop(0, 16, finish, 0)

    def collect_diagonal(i, carry):
        @pl.when(jnp.logical_not(is_self(i)))
        def _():
            pltpu.make_async_remote_copy(
                src_ref=dsend.at[0], dst_ref=drecv.at[i], send_sem=ds_sem.at[0],
                recv_sem=dr_sem.at[i], device_id=sibling).wait_recv()
        return carry

    lax.fori_loop(0, 16, collect_diagonal, 0)
    total = drecv[0].astype(F32)
    for i in range(1, 16):
        total = total + drecv[i].astype(F32)
    out_ref[0, :, column(mine)] = total

    for j in range(1, 4):
        receive_block(j)

    @pl.when(mine >= 4)
    def _():
        receive_block(4)

    for j in range(1, 4):
        for e in range(2):
            x_copy(j, e).wait_send()

    @pl.when(mine < 4)
    def _():
        for e in range(2):
            x_copy(4, e).wait_send()

    def finish_diagonal(i, carry):
        @pl.when(jnp.logical_not(is_self(i)))
        def _():
            d_copy(i).wait_send()
        return carry

    lax.fori_loop(0, 16, finish_diagonal, 0)


def hand_over(matrix_ref, vector_ref, out_ref, vec_ref):
    out_ref[...] = matrix_ref[...]
    vec_ref[...] = vector_ref[...]


def local(
    global_deriv,
    local_deriv,
    hit_weight,
    hit_resid,
    block_ids,
    hit_count,
    track_region,
    block_place,
):
    vmem = pl.BlockSpec(memory_space=pltpu.VMEM)
    dma = pltpu.SemaphoreType.DMA
    matrix, vector = pl.pallas_call(
        kernel,
        name="assemble",
        out_shape=(
            jax.ShapeDtypeStruct((1, ROWS, WIDTH), F32),
            jax.ShapeDtypeStruct((1, ROWS), F32),
        ),
        in_specs=[pl.BlockSpec(memory_space=pltpu.SMEM), pl.BlockSpec(memory_space=pl.ANY)] + [vmem] * 6,
        out_specs=(vmem, vmem),
        scratch_shapes=[
            pltpu.VMEM((TRK, HITS, BS), BF16),
            dma,
            pltpu.SMEM((1, N_REGION * CAP), jnp.int32),
            pltpu.VMEM((BR, N_REGION * CAP), jnp.int32),
            pltpu.VMEM((14, 3, GROUP, HITS, BS), BF16),
            pltpu.VMEM((CHUNKS, 3, GROUP, HITS, BS), BF16),
            pltpu.VMEM((14, 3, GROUP, 256), BF16),
            pltpu.VMEM((CHUNKS, 3, GROUP, 256), BF16),
            pltpu.VMEM((TRK, 256), BF16),
            pltpu.VMEM((WIDTH, HALF * HITS), BF16),
            pltpu.VMEM((CHUNKS, BR, HALF * HITS), BF16),
            pltpu.VMEM((CHUNKS * 120, WIDTH + WIDTH // 2), BF16),
            pltpu.VMEM((4, 256, 768), F32),
            pltpu.VMEM((WIDTH, BS), F32),
            pltpu.VMEM((BR, BS), F32),
            pltpu.VMEM((BR, 1, BS), F32),
            pltpu.VMEM((16, 4, ROWS, BS), BF16),
            pltpu.VMEM((16, 4, ROWS, BS), BF16),
            pltpu.VMEM((16, 1, BS), F32),
            pltpu.VMEM((16, ROWS, BS), BF16),
            pltpu.VMEM((16, ROWS, BS), BF16),
            pltpu.VMEM((8, 32, BS), BF16),
            pltpu.VMEM((8, 32, BS), BF16),
            dma((14, 3)), dma((16, 3)), dma((14,)), dma((16,)),
            dma((16,)), dma((16,)), dma((16,)), dma((16,)), dma((16,)), dma((16,)), dma((8,)), dma((8,)), dma,
            pltpu.SemaphoreType.REGULAR, pltpu.SemaphoreType.REGULAR, pltpu.SemaphoreType.REGULAR,
        ],
        compiler_params=pltpu.CompilerParams(
            collective_id=0, has_side_effects=True, vmem_limit_bytes=56 << 20),
    )(
        block_place, global_deriv, local_deriv.transpose(1, 2, 0), hit_weight.T, hit_resid.T,
        block_ids.T, hit_count.reshape(1, TRK), track_region.reshape(1, TRK))
    return pl.pallas_call(
        hand_over,
        name="hand_over",
        out_shape=(
            jax.ShapeDtypeStruct((1, ROWS, WIDTH), F32),
            jax.ShapeDtypeStruct((1, ROWS), F32),
        ),
        in_specs=[vmem, vmem],
        out_specs=(vmem, vmem),
    )(matrix, vector)


def solution(mesh):
    return jax.shard_map(
        local,
        mesh=mesh,
        in_specs=(
            P(("region", "tile"), None, None),
            P(("region", "tile"), None, None),
            P(("region", "tile"), None),
            P(("region", "tile"), None),
            P(("region", "tile"), None),
            P(("region", "tile")),
            P(("region", "tile"), None),
            P(),
        ),
        out_specs=(P("region", "tile", None), P("region", "tile")),
        check_vma=False,
    )
```
